32 devices in a mesh: dp: 8 (over z, x), mp: 4 (over y, core).
Axes of the slice: x: 2, y: 2, z: 4, core: 2. Of those that a mesh axis runs over, the one named last changes fastest.
Arguments:
- patches: bfloat16 [9216, 3072], P('dp'), may hold values from -6 to 6
- weight: bfloat16 [3072, 1536], P(None, 'mp'), may hold values from -0.109375 to 0.109375
- conv_bias: float32 [1536], P('mp'), may hold values from -3 to 3
- cotangent: bfloat16 [9216, 1536], P('dp', 'mp'), may hold values from -0.0390625 to 0.0390625
- row_scale: float32 [3072], replicated, may hold values from 0.25 to 4
- col_scale: float32 [1536], P('mp'), may hold values from 0.25 to 4
Outputs:
- output: bfloat16 [9216, 1536], P('dp', 'mp')
- left_factor: float32 [3072, 3072], P('dp', 'mp')
- right_factor: float32 [1536, 1536], P('dp', 'mp')
- norm_pair: float32 [2], replicated
The draws below stay inside these ranges and needn't reach their ends.
All inputs are finite; a program needn't handle non-finite values.
Results may differ from the reference program's by a relative error of at most 0.001.
Values sent between devices are 32-bit elements; how exact they have to be, the bound alone decides.
A program may use at most 64 MiB of HBM per device.

```python
import math
import jax
import jax.numpy as jnp
from jax import lax

COUT = 1536
K = 3072
ROWS_DEV = 1152
ROWS = 9216
N_DP = 8


def draw_cotangent(key, part):
    row_index = jnp.arange(ROWS).astype(jnp.float32)
    row_ramp = ((1.0 + 2.0 * row_index / (ROWS - 1)) * 0.5 * ROWS ** (-0.5))[:, None]
    first_key = jax.random.fold_in(key, 0)
    third_key = jax.random.fold_in(key, 2)
    edge_value = 3.75 * ROWS ** (-0.5)
    edge_signs = jnp.where(jax.random.uniform(third_key, (1, COUT), jnp.float32) < 0.5, -1.0, 1.0)
    values = jnp.clip(jax.random.normal(first_key, (ROWS, COUT), jnp.float32), -4.9, 4.9) * row_ramp
    values = jnp.clip(values, -edge_value, edge_value)
    last_row = (row_index == ROWS - 1)[:, None]
    values = jnp.where(last_row, edge_signs * edge_value, values)
    return values.astype(jnp.bfloat16)


def raised(entries, key, source, target, blocks, factor):
    owner, partner = [(jnp.arange(entries.shape[axis_at]) // (entries.shape[axis_at] // blocks)).reshape([-1 if axis == axis_at else 1 for axis in range(entries.ndim)]) for axis_at in (source, target)]
    chosen = jax.random.permutation(key, blocks)[partner]
    strong = (owner == chosen) | (owner == (partner + blocks // 2) % blocks)
    return jnp.where(strong, factor * entries, entries)


def steps_of(rng, extent, shards, smallest, high):
    factor_of, own = 1.0, jax.random.fold_in(rng, 6)
    for axis_at, parts in shards:
        steps = jnp.exp(jax.random.uniform(jax.random.fold_in(own, axis_at), (parts,), jnp.float32, smallest / len(shards), high / len(shards)))
        factor_of = factor_of * jnp.repeat(steps, extent[axis_at] // parts).reshape([-1 if axis == axis_at else 1 for axis in range(len(extent))])
    return factor_of


def scatter_about(stream_key, extent, scale, reach, cuts=(), kind=jnp.bfloat16):
    result = scale * jax.random.normal(stream_key, extent, jnp.float32)
    if cuts:
        result = result * steps_of(stream_key, extent, cuts, -0.22, 0.18)
    return jnp.clip(result, -reach, reach).astype(kind)


def heavy_noise(rng, shape, spread, most, shards, heavy, held_as=jnp.bfloat16):
    drawn = spread * jax.random.normal(rng, shape, jnp.float32)
    if shards:
        drawn = drawn * steps_of(rng, shape, shards, -0.22, 0.18)
    return jnp.clip(raised(drawn, jax.random.fold_in(rng, 3), *heavy), -most, most).astype(held_as)


def setup_inputs(seed: int = 0) -> dict:
    arg_keys = jax.random.split(jax.random.key(seed), 7)
    return {
        "patches": heavy_noise(arg_keys[0], (ROWS, K), 1.0, 6.0, ((0, 8),), (0, 1, 8, 2.0)),
        "weight": scatter_about(arg_keys[1], (K, COUT), K ** -0.5, 0.109375, ((1, 4),)),
        "conv_bias": scatter_about(arg_keys[2], (COUT,), 0.5, 3.0, ((0, 4),), jnp.float32),
        "cotangent": draw_cotangent(jax.random.fold_in(arg_keys[6], 71), 0),
        "row_scale": jnp.clip(jnp.exp(jax.random.uniform(arg_keys[4], (K,), jnp.float32, math.log(0.25), math.log(4.0))), 0.25, 4.0),
        "col_scale": jnp.clip(jnp.exp(math.log(4.0) - 2.7725887 * jax.random.uniform(arg_keys[5], (COUT,), jnp.float32) ** steps_of(arg_keys[5], (COUT,), ((0, 4),), -0.2, 0.2)), 0.25, 4.0),
    }


def reference(patches, weight, conv_bias, cotangent, row_scale, col_scale):
    output = (jnp.dot(patches, weight, preferred_element_type=jnp.float32) + conv_bias).astype(jnp.bfloat16)
    inner_width = patches.shape[1]
    out_cols = cotangent.shape[1]
    patch_blocks = patches.reshape(N_DP, ROWS_DEV, inner_width)
    tangents = cotangent.reshape(N_DP, ROWS_DEV, out_cols)
    scale_grid = row_scale[:, None] * col_scale[None, :]

    def accumulate(running, block_pair):
        grad_sum, small_sum = running
        local_grad = lax.dot_general(block_pair[0], block_pair[1], (((0,), (0,)), ((), ())), preferred_element_type=jnp.float32)
        weighted = local_grad * scale_grid
        return (grad_sum + local_grad, small_sum + jnp.sum(weighted * weighted)), None

    starting = (jnp.zeros((inner_width, out_cols), jnp.float32), jnp.zeros((), jnp.float32))
    (gradient, small_sum), _ = lax.scan(accumulate, starting, (patch_blocks, tangents))
    left_factor = jnp.dot(gradient, gradient.T, precision=lax.Precision.HIGHEST, preferred_element_type=jnp.float32) / COUT
    right_factor = jnp.dot(gradient.T, gradient, precision=lax.Precision.HIGHEST, preferred_element_type=jnp.float32) / K
    weighted = gradient * scale_grid
    large_sum = jnp.sum(weighted * weighted)
    norm_pair = jnp.stack([small_sum, large_sum]) / (K * COUT)
    return output, left_factor, right_factor, norm_pair
```

```python
import functools

import jax
import jax.numpy as jnp
from jax import lax
from jax.experimental import pallas as pl
from jax.experimental.pallas import tpu as pltpu
from jax.sharding import PartitionSpec as P

COUT = 1536
K = 3072
F32 = jnp.float32
BF16 = jnp.bfloat16
MESH = pl.DeviceIdType.MESH


def shards(patches, weight, conv_bias, cotangent, row_scale, col_scale):
    output = (jnp.dot(patches, weight, preferred_element_type=jnp.float32) + conv_bias).astype(
        jnp.bfloat16
    )
    inner_width = patches.shape[1]
    strip_rows = inner_width // lax.axis_size("dp")
    local_grad = lax.dot_general(
        patches, cotangent, (((0,), (0,)), ((), ())), preferred_element_type=jnp.float32
    )
    weighted = local_grad * row_scale[:, None] * col_scale[None, :]
    small_sum = jnp.sum(weighted * weighted)
    column = lax.psum(local_grad, "dp")
    rows_here = lax.dynamic_slice_in_dim(column, lax.axis_index("dp") * strip_rows, strip_rows, 0)
    left_part = lax.dot_general(
        rows_here,
        column,
        (((1,), (1,)), ((), ())),
        precision=lax.Precision.HIGHEST,
        preferred_element_type=jnp.float32,
    )
    left_factor = lax.psum_scatter(left_part / COUT, "mp", scatter_dimension=1, tiled=True)
    full_strip = lax.all_gather(rows_here, "mp", axis=1, tiled=True)
    right_factor = lax.psum_scatter(
        lax.dot_general(
            full_strip,
            rows_here,
            (((0,), (0,)), ((), ())),
            precision=lax.Precision.HIGHEST,
            preferred_element_type=jnp.float32,
        )
        / K,
        "dp",
        scatter_dimension=0,
        tiled=True,
    )
    row_part = lax.dynamic_slice_in_dim(row_scale, lax.axis_index("dp") * strip_rows, strip_rows, 0)
    scaled_rows = rows_here * row_part[:, None] * col_scale[None, :]
    large_sum = jnp.sum(scaled_rows * scaled_rows)
    small_total, large_total = lax.psum((small_sum, large_sum), ("dp", "mp"))
    norm_pair = jnp.stack([small_total, large_total]) / (K * COUT)
    return (output, left_factor, right_factor, norm_pair)


def flip(bit, by):
    return 1 - bit if by else bit


def halves(value):
    high = value.astype(BF16)
    return high, (value - high.astype(F32)).astype(BF16)


def dot3(a, b, dims):
    a_high, a_low = a
    b_high, b_low = b
    dot = functools.partial(
        lax.dot_general, dimension_numbers=(dims, ((), ())), preferred_element_type=F32
    )
    return dot(a_high, b_high) + (dot(a_high, b_low) + dot(a_low, b_high))


GROUPS = (128, 128, 128)
LEVELS = (1, 2, 3)
OUTER = (
    (1, 2, 3), (1, 1, 3), (2, 0, 3), (2, 0, 2), (1, 1, 2), (2, 0, 1), (14, 0), (2, 2, 3), (14, 1), (3, 0),
    (4, 0), (1, 2, 2), (15, 0), (2, 1, 3), (11, 0, 0, 0), (8, 0, 0), (2, 1, 2), (1, 1, 1), (6, 0, 1),
    (1, 2, 1), (14, 2), (1, 1, 0), (14, 3), (2, 2, 2), (6, 0, 2), (11, 0, 0, 2), (5, 0), (11, 0, 0, 1),
    (15, 1), (12, 0, 0, 1), (9, 0, 0), (2, 1, 1), (6, 0, 3), (11, 0, 0, 3), (8, 0, 3), (1, 2, 0), (2, 2, 1),
    (3, 1), (5, 1), (8, 0, 1), (4, 1), (8, 1, 0), (9, 1, 0), (7, 0), (11, 1, 0, 0), (12, 0, 0, 2),
    (11, 1, 0, 3), (12, 0, 0, 0), (11, 0, 1, 0), (3, 2), (12, 1, 0, 0), (4, 2), (11, 1, 0, 2), (12, 0, 0, 3),
    (8, 2, 0), (9, 2, 0), (5, 2), (9, 0, 3), (6, 1, 1), (11, 0, 2, 0), (7, 1), (12, 1, 0, 3), (8, 1, 1),
    (12, 0, 1, 0), (9, 1, 1), (6, 2, 1), (11, 1, 1, 0), (8, 2, 1), (12, 0, 2, 0), (9, 2, 1), (7, 2), (16, 0),
    (11, 1, 2, 0), (8, 0, 2), (6, 1, 2), (11, 0, 1, 2), (12, 1, 1, 0), (12, 1, 0, 2), (16, 1), (11, 1, 2, 1),
    (8, 1, 2), (11, 0, 1, 1), (11, 1, 1, 2), (12, 1, 2, 0), (6, 2, 2), (11, 1, 2, 2), (11, 1, 1, 1),
    (12, 1, 1, 1), (11, 1, 0, 1), (8, 2, 2), (12, 1, 0, 1), (12, 1, 2, 1), (12, 1, 1, 2), (11, 0, 2, 1),
    (11, 0, 2, 2), (16, 2), (12, 1, 2, 2), (6, 1, 3), (11, 1, 1, 3), (11, 0, 1, 3), (6, 2, 3), (12, 1, 1, 3),
    (11, 1, 2, 3), (12, 1, 2, 3), (13, 1, 1), (12, 0, 1, 1), (9, 0, 2), (11, 0, 2, 3), (13, 1, 2), (13, 1, 0),
    (9, 1, 2), (9, 2, 2), (8, 1, 3), (12, 0, 2, 1), (9, 1, 3), (13, 0, 0), (8, 2, 3), (9, 2, 3), (16, 3),
    (9, 0, 1), (10,), (12, 0, 1, 3), (12, 0, 2, 2), (12, 0, 2, 3), (12, 0, 1, 2), (16, 4), (15, 2),
    (13, 0, 1), (13, 0, 2), (17,),
)
INNER = (
    (1, 1, 1), (1, 1, 2), (1, 1, 3), (2, 0, 3), (1, 2, 3), (15, 0), (2, 0, 2), (1, 2, 1), (1, 2, 2), (14, 0),
    (2, 0, 1), (3, 0), (14, 1), (5, 0), (4, 0), (1, 1, 0), (11, 0, 0, 0), (6, 0, 2), (6, 0, 1), (2, 1, 3),
    (8, 0, 2), (6, 0, 3), (11, 0, 0, 3), (2, 2, 3), (8, 0, 0), (11, 0, 0, 1), (14, 2), (12, 0, 0, 0),
    (1, 2, 0), (14, 3), (2, 1, 2), (8, 0, 1), (9, 0, 2), (2, 1, 1), (8, 0, 3), (11, 0, 0, 2), (9, 0, 1),
    (2, 2, 1), (2, 2, 2), (7, 0), (11, 1, 0, 1), (11, 1, 0, 3), (11, 1, 0, 2), (9, 0, 0), (3, 1), (4, 1),
    (12, 0, 0, 3), (12, 0, 0, 2), (12, 1, 0, 1), (5, 1), (11, 0, 1, 0), (12, 1, 0, 3), (3, 2), (4, 2),
    (16, 0), (12, 0, 1, 0), (5, 2), (6, 1, 1), (8, 1, 0), (6, 1, 2), (12, 1, 0, 2), (16, 1), (11, 0, 1, 1),
    (7, 1), (11, 1, 1, 0), (11, 1, 1, 1), (12, 0, 1, 1), (6, 2, 1), (11, 1, 1, 2), (6, 2, 2), (8, 2, 2),
    (11, 0, 2, 0), (11, 0, 2, 2), (8, 1, 2), (9, 1, 2), (12, 1, 1, 0), (6, 1, 3), (11, 1, 1, 3), (8, 1, 1),
    (7, 2), (11, 1, 2, 1), (11, 1, 2, 0), (12, 1, 1, 1), (9, 1, 1), (8, 1, 3), (11, 0, 1, 2), (12, 1, 2, 1),
    (6, 2, 3), (12, 1, 1, 3), (11, 1, 2, 3), (9, 0, 3), (16, 2), (8, 2, 3), (9, 2, 2), (11, 0, 1, 3),
    (9, 1, 0), (12, 0, 0, 1), (9, 1, 3), (12, 0, 2, 0), (12, 1, 1, 2), (8, 2, 1), (11, 0, 2, 1), (13, 1, 1),
    (12, 1, 2, 0), (9, 2, 3), (9, 2, 1), (8, 2, 0), (9, 2, 0), (11, 1, 2, 2), (12, 1, 2, 2), (16, 3),
    (12, 0, 1, 2), (10,), (11, 0, 2, 3), (12, 1, 2, 3), (12, 0, 2, 1), (13, 1, 2), (12, 0, 1, 3),
    (11, 1, 0, 0), (12, 1, 0, 0), (15, 1), (12, 0, 2, 2), (13, 0, 0), (12, 0, 2, 3), (13, 0, 1), (13, 1, 0),
    (16, 4), (15, 2), (13, 0, 2), (17,),
)

def bounds():
    at = [0]
    for rows in GROUPS:
        at.append(at[-1] + rows)
    return at


def spans_of():
    at = bounds()
    edges = [0] + [at[n] for n in LEVELS]
    spans, levels = [], []
    for low, high in zip(edges[:-1], edges[1:]):
        level = [len(spans)]
        spans.append(((low, high - low), (0, high)))
        if low:
            level.append(len(spans))
            spans.append(((0, low), (low, high - low)))
        levels.append(level)
    return spans, levels


def kernel(
    patches_in, weight_in, bias_in, cot, row_scale, col_scale, output_out, left, right, norms, *scratch
):
    (
        grad, got_x, got_p, got_i, column, other, csplit, osplit, bcol, racc, rgot, nown, ngot,
        s_x, r_x, s_p, r_p, s_i, r_i, s_o, r_o, s_gp, s_gi, r_g,
        s_lc, r_lc, s_ly, r_ly, s_v, r_v, s_b1, s_b2, r_b, s_r, r_r, s_n, r_n,
        patches, weight, output, load, w_load, o_store,
    ) = scratch[:43]
    spans, levels = spans_of()
    edges = [0] + [bounds()[n] for n in LEVELS]
    count = len(spans)
    parts, cores, over_y = (scratch[43 + i * count:43 + (i + 1) * count] for i in range(3))
    d, m = lax.axis_index("dp"), lax.axis_index("mp")
    x, z = d % 2, d // 2
    z0, z1 = z % 2, z // 2
    c, y = m % 2, m // 2
    zs = (z, z + 1 - 2 * z0, 2 - z1, 3 - 3 * z1)
    px = (d + 1 - 2 * x, m)
    pz = (zs[1] * 2 + x, m)
    pi = ((3 - z) * 2 + x, m)
    pc = (d, m + 1 - 2 * c)
    py = (d, m + 2 - 4 * y)
    inner = (z0 + z1) % 2 == 1
    outer = (z0 + z1) % 2 == 0
    source = m == z
    relay = py[1] == z
    size = rgot.shape[1]
    half = rgot.shape[0]
    at = bounds()
    H = len(GROUPS)
    groups = [pl.ds(at[h], GROUPS[h]) for h in range(H)]

    def strip_at(k, opposite):
        return zs[k] * 2 + (1 - x if opposite else x)

    def strip(k, opposite):
        return pl.ds(pl.multiple_of(strip_at(k, opposite) * size, size), size)

    def strip_group(k, opposite, h):
        first = pl.multiple_of(strip_at(k, opposite) * size + at[h], 32)
        return pl.ds(first, GROUPS[h])

    def copy(src, dst, send, recv, to):
        return pltpu.make_async_remote_copy(
            src_ref=src, dst_ref=dst, send_sem=send, recv_sem=recv, device_id=to, device_id_type=MESH
        )

    barrier = pltpu.get_barrier_semaphore()
    for to in (px, pz, pi, pc, py):
        pl.semaphore_signal(barrier, inc=1, device_id=to, device_id_type=MESH)
    FAR = (3, 2, 1, 0)
    for o in (1, 0):
        for k in FAR:
            rows = strip(k, o)
            pltpu.make_async_copy(
                patches_in.at[:, rows], patches.at[:, rows], load.at[2 * k + o]
            ).start()
    weight_load = pltpu.make_async_copy(weight_in, weight, w_load)
    weight_load.start()
    out_copy = pltpu.make_async_copy(output, output_out, o_store)
    nown[...] = jnp.zeros_like(nown)
    racc[...] = jnp.zeros_like(racc)
    pl.semaphore_wait(barrier, 5)
    bias = bias_in[...].reshape(1, size)
    col_row = col_scale[...].reshape(1, size)
    col_square = col_row * col_row

    def folded(value, index):
        square = value * value * col_square
        total = jnp.zeros((1, size), F32)
        for b in range(size // 128):
            scale = row_scale[pl.ds(index * (size // 128) + b, 1), :]
            total += dot3(
                halves(scale * scale), halves(square[b * 128:(b + 1) * 128]), ((1,), (0,))
            )
        return total

    def col(k, h):
        return column.at[zs[k], groups[h]]

    hk = [(h, k) for h in range(H) for k in range(4)]
    xc = {
        (h, k): copy(
            grad.at[strip_group(k, 1, h)], got_x.at[k, groups[h]], s_x.at[4 * h + k], r_x.at[4 * h + k], px
        )
        for h, k in hk
    }
    to_p = {
        (h, k): copy(
            got_x.at[k, groups[h]], got_p.at[k - 1, groups[h]],
            s_p.at[3 * h + k - 1], r_p.at[3 * h + k - 1], pz,
        )
        for h, k in hk if k
    }
    to_i = {
        (h, k): copy(
            got_x.at[k, groups[h]], got_i.at[k - 2, groups[h]],
            s_i.at[2 * h + k - 2], r_i.at[2 * h + k - 2], pi,
        )
        for h, k in hk if k >= 2
    }

    def pass_on(k, h, index, send, to):
        return copy(col(k, h), col(k, h), send, r_g.at[4 * h + index], to)

    gp = {
        (h, j): pass_on((0, 2, 3)[j], h, j + 1, s_gp.at[3 * h + j], pz)
        for h in range(H) for j in range(3)
    }
    gi = {
        (h, j): pass_on(j, h, j + 2, s_gi.at[2 * h + j], pi) for h in range(H) for j in range(2)
    }
    g_in = {(h, k): pass_on(k, h, k, s_gp.at[0], pz) for h, k in hk if k}
    o_copy = [copy(col(0, h), other.at[groups[h]], s_o.at[h], r_o.at[h], px) for h in range(H)]

    def b_copy(src, h, k, send, to):
        return copy(src, bcol.at[k, groups[h]], send.at[4 * h + k], r_b.at[4 * h + k], to)

    b_core = {(h, k): b_copy(col(k, h), h, k, s_b1, pc) for h, k in hk}
    b_y = {(h, k): b_copy(col(k, h), h, k, s_b2, py) for h, k in hk}
    b_on = {(h, k): b_copy(bcol.at[k, groups[h]], h, k, s_b1, pc) for h, k in hk}
    wpk = [(w, p, k) for w in range(2) for p in range(count) for k in range(4)]
    lcc = {
        (w, p, k): copy(
            parts[p].at[w, k], cores[p].at[w, k],
            s_lc.at[(w * count + p) * 4 + k], r_lc.at[(w * count + p) * 4 + k], pc,
        )
        for w, p, k in wpk
    }
    lyc = {
        (w, p, k): copy(
            parts[p].at[w, k], over_y[p].at[w], s_ly.at[w * count + p], r_ly.at[w * count + p], py
        )
        for w, p, k in wpk
    }
    at_k = 0
    for k in range(1, 4):
        at_k = at_k + k * (zs[k] == m).astype(jnp.int32)
    left_at = pl.multiple_of(x * size, size)

    def place(p):
        (row, rows), (first, cols) = spans[p]
        return left.at[pl.ds(row, rows), pl.ds(pl.multiple_of(left_at + first, 128), cols)]

    vc = [copy(over_y[p].at[1], place(p), s_v.at[p], r_v.at[p], px) for p in range(count)]
    rc = copy(racc.at[pl.ds(pl.multiple_of((1 - x) * half, half), half)], rgot, s_r, r_r, px)
    n_to = (pc, pz, pi, py, px)
    nc = [copy(nown.at[i], ngot.at[i], s_n.at[i], r_n.at[i], n_to[i]) for i in range(5)]

    def split(value, ref, g):
        high, low = halves(value)
        ref[0, g, :] = high
        ref[1, g, :] = low

    def zs_dynamic(k):
        low, high = k % 2, k // 2
        near = z + low - 2 * z0 * low
        beyond = 2 - z1 + low * (1 - 2 * z1)
        return near + high * (beyond - near)

    def make_grad(i, _):
        k, opposite = 3 - i % 4, 1 - i // 4
        index = zs_dynamic(k) * 2 + x + opposite - 2 * x * opposite
        rows = pl.ds(pl.multiple_of(index * size, size), size)
        pltpu.make_async_copy(
            patches_in.at[:, rows], patches.at[:, rows], load.at[2 * k + opposite]
        ).wait()
        grad[rows, :] = lax.dot_general(
            patches[:, rows], cot[...], (((0,), (0,)), ((), ())), preferred_element_type=F32
        )

        @pl.when(opposite == 1)
        def _():
            first = pl.ds(pl.multiple_of(index * size, size), GROUPS[0])
            copy(grad.at[first], got_x.at[k, groups[0]], s_x.at[k], r_x.at[k], px).start()

        return 0

    def xs(inside, h, k):
        xc[h, k].start()

    def rs(inside, h, k):
        g = groups[h]
        xc[h, k].wait_recv()
        value = got_x[k, g, :] + grad[strip_group(k, 0, h), :]
        if inside and k >= 2:
            to_p[h, k].wait_recv()
            value += got_p[k - 1, g, :]
        if inside and k == 1:
            to_i[h, 3].wait_recv()
            value += got_i[1, g, :]
        got_x[k, g, :] = value
        (to_i if inside and k >= 2 else to_p)[h, k].start()

    def own0(inside, h):
        g = groups[h]
        xc[h, 0].wait_recv()
        to_p[h, 1].wait_recv()
        value = got_x[0, g, :] + grad[strip_group(0, 0, h), :] + got_p[0, g, :]
        if inside:
            to_i[h, 2].wait_recv()
            value += got_i[0, g, :]
        column[z, g, :] = value
        split(value, csplit.at[:, 0], g)

    def own(inside, h):
        gp[h, 0].start()
        if inside:
            gi[h, 0].start()

    def os(inside, h):
        o_copy[h].start()

    def ar(inside, h, k):
        g_in[h, k].wait_recv()
        if inside:
            (gi[h, 1] if k == 1 else gp[h, k - 1]).start()
        split(column[zs[k], groups[h], :], csplit.at[:, k], groups[h])

    def oth(inside, h):
        o_copy[h].wait_recv()
        split(other[groups[h], :], osplit, groups[h])

    def bs(inside, h, k):
        @pl.when(source)
        def _():
            b_y[h, k].start()
            b_core[h, k].start()
            bcol[k, groups[h], :] = column[zs[k], groups[h], :]

        @pl.when(jnp.logical_not(source))
        def _():
            b_core[h, k].wait_recv()

        @pl.when(relay)
        def _():
            b_on[h, k].start()

    def rt(inside, level, k):
        g = pl.ds(edges[level], edges[level + 1] - edges[level])
        racc[...] += dot3(
            halves(bcol[k, g, :]), (csplit[0, k, g, :], csplit[1, k, g, :]), ((0,), (0,))
        )

    def start_rc(inside):
        rc.start()

    def lu(inside, w, level, k):
        mine = osplit if w else csplit.at[:, 0]
        for p in levels[level]:
            (row, rows), (first, cols) = spans[p]
            g, f = pl.ds(row, rows), pl.ds(first, cols)
            parts[p][w, k] = dot3(
                (mine[0, g, :], mine[1, g, :]), (csplit[0, k, f, :], csplit[1, k, f, :]), ((1,), (1,))
            )

        @pl.when(zs[k] % 2 != c)
        def _():
            for p in levels[level]:
                lcc[w, p, k].start()

    def rd(inside, w, level, k):
        @pl.when(zs[k] % 2 == c)
        def _():
            for p in levels[level]:
                lcc[w, p, k].wait_recv()
                parts[p][w, k] += cores[p][w, k]

            @pl.when(zs[k] // 2 != y)
            def _():
                for p in levels[level]:
                    lyc[w, p, k].start()

    def fi(inside, w, level):
        for p in levels[level]:
            lyc[w, p, 0].wait_recv()
            total = (parts[p][w, at_k] + over_y[p][w]) * (1.0 / COUT)
            if w:
                over_y[p][1] = total
                vc[p].start()
            else:
                place(p)[...] = total

    def small_step(s, _):
        rows = pl.ds(pl.multiple_of(s * size, size), size)
        nown[0, 0:1, :] += folded(grad[rows, :], s)
        return 0

    def small(inside, i):
        lax.fori_loop(2 * i, 2 * i + 2, small_step, 0)

    def out_step(i, _):
        rows = pl.ds(pl.multiple_of(i * 128, 128), 128)
        value = jnp.dot(patches[rows, :], weight[...], preferred_element_type=F32) + bias
        output[rows, :] = value.astype(BF16)
        return 0

    tiles = patches.shape[0] // 128
    cuts = (0, tiles // 3, 2 * (tiles // 3), tiles)

    def out(inside, i):
        if i == 0:
            weight_load.wait()
        lax.fori_loop(cuts[i], cuts[i + 1], out_step, 0)
        if i == 2:
            out_copy.start()

    def nm(inside, i):
        if i == 0:
            nown[0, 8:9, :] = folded(column[z], strip_at(0, 0))
        else:
            nc[i - 1].wait_recv()
            nown[i] = nown[i - 1] + ngot[i - 1]
        nc[i].start()

    def finish(inside):
        nc[4].wait_recv()
        both = nown[4] + ngot[4]
        norms[0] = jnp.sum(both[0:8]) / (K * COUT)
        norms[1] = jnp.sum(both[8:16]) / (K * COUT)
        rc.wait_recv()
        right[...] = (racc[pl.ds(pl.multiple_of(x * half, half), half), :] + rgot[...]) * (1.0 / K)
        for one in vc:
            one.wait_recv()
        out_copy.wait()

    lax.fori_loop(0, 8, make_grad, 0)
    steps = (None, xs, rs, own0, own, os, ar, oth, bs, rt, start_rc, lu, rd, fi, small, out, nm, finish)

    @pl.when(outer)
    def _():
        for code, *where in OUTER:
            steps[code](False, *where)

    @pl.when(inner)
    def _():
        for code, *where in INNER:
            steps[code](True, *where)

    sent = [*xc.values(), *o_copy, *vc, rc, *nc]
    for h in range(H):
        sent += [to_p[h, 1], gp[h, 0]]
    for w in range(2):
        for p in range(count):
            sent.append(lyc[w, p, 0])
    for one in sent:
        one.wait_send()

    @pl.when(outer)
    def _():
        for h in range(H):
            to_p[h, 2].wait_send()
            to_p[h, 3].wait_send()

    @pl.when(inner)
    def _():
        for h in range(H):
            for one in (to_i[h, 2], to_i[h, 3], gp[h, 1], gp[h, 2], gi[h, 0], gi[h, 1]):
                one.wait_send()

    @pl.when(source)
    def _():
        for key in hk:
            b_y[key].wait_send()
            b_core[key].wait_send()

    @pl.when(relay)
    def _():
        for key in hk:
            b_on[key].wait_send()

    for k in range(4):

        @pl.when(zs[k] % 2 != c)
        def _():
            for w in range(2):
                for p in range(count):
                    lcc[w, p, k].wait_send()


def deliver_kernel(output_in, left_in, right_in, norms_in, output, left, right, norms, sems):
    norms[0] = norms_in[0]
    norms[1] = norms_in[1]
    pairs = ((output_in, output), (left_in, left), (right_in, right))
    copies = [pltpu.make_async_copy(a, b, sems.at[i]) for i, (a, b) in enumerate(pairs)]
    for one in copies:
        one.start()
    for one in copies:
        one.wait()


def deliver(results):
    vmem = pl.BlockSpec(memory_space=pltpu.VMEM)
    hbm = pl.BlockSpec(memory_space=pl.ANY)
    smem = pl.BlockSpec(memory_space=pltpu.SMEM)
    return pl.pallas_call(
        deliver_kernel,
        out_shape=tuple(jax.ShapeDtypeStruct(r.shape, r.dtype) for r in results),
        in_specs=[vmem, vmem, vmem, smem],
        out_specs=(hbm, hbm, hbm, smem),
        scratch_shapes=[pltpu.SemaphoreType.DMA((3,))],
    )(*results)


def fused(patches, weight, conv_bias, cotangent, row_scale, col_scale):
    rows, width = patches.shape
    cols = cotangent.shape[1]
    size = width // 8
    H = len(GROUPS)
    vmem = pl.BlockSpec(memory_space=pltpu.VMEM)
    hbm = pl.BlockSpec(memory_space=pl.ANY)
    dma = pltpu.SemaphoreType.DMA
    one = dma
    spans, _ = spans_of()
    count = len(spans)
    shapes = [(a[1], b[1]) for a, b in spans]
    results = pl.pallas_call(
        kernel,
        out_shape=(
            jax.ShapeDtypeStruct((rows, cols), BF16),
            jax.ShapeDtypeStruct((size, width // 4), F32),
            jax.ShapeDtypeStruct((cols // 2, cols), F32),
            jax.ShapeDtypeStruct((2,), F32),
        ),
        in_specs=[hbm, hbm, vmem, vmem, vmem, vmem],
        out_specs=(hbm, vmem, vmem, pl.BlockSpec(memory_space=pltpu.SMEM)),
        scratch_shapes=[
            pltpu.VMEM((width, cols), F32),
            pltpu.VMEM((4, size, cols), F32),
            pltpu.VMEM((3, size, cols), F32),
            pltpu.VMEM((2, size, cols), F32),
            pltpu.VMEM((4, size, cols), F32),
            pltpu.VMEM((size, cols), F32),
            pltpu.VMEM((2, 4, size, cols), BF16),
            pltpu.VMEM((2, size, cols), BF16),
            pltpu.VMEM((4, size, cols), F32),
            pltpu.VMEM((cols, cols), F32),
            pltpu.VMEM((cols // 2, cols), F32),
            pltpu.VMEM((5, 16, cols), F32),
            pltpu.VMEM((5, 16, cols), F32),
            dma((4 * H,)), dma((4 * H,)), dma((3 * H,)), dma((3 * H,)), dma((2 * H,)), dma((2 * H,)),
            dma((H,)), dma((H,)), dma((3 * H,)), dma((2 * H,)), dma((4 * H,)),
            dma((8 * count,)), dma((8 * count,)), dma((2 * count,)), dma((2 * count,)),
            dma((count,)), dma((count,)),
            dma((4 * H,)), dma((4 * H,)), dma((4 * H,)), one, one,
            dma((5,)), dma((5,)),
            pltpu.VMEM((rows, width), BF16),
            pltpu.VMEM((width, cols), BF16),
            pltpu.VMEM((rows, cols), BF16),
            dma((8,)), one, one,
            *[pltpu.VMEM((2, 4, *shape), F32) for shape in shapes],
            *[pltpu.VMEM((2, 4, *shape), F32) for shape in shapes],
            *[pltpu.VMEM((2, *shape), F32) for shape in shapes],
        ],
        compiler_params=pltpu.CompilerParams(
            collective_id=0, has_side_effects=True, vmem_limit_bytes=61 * 1024 * 1024
        ),
    )(
        patches, weight, conv_bias, cotangent, row_scale.reshape(-1, 128), col_scale
    )
    return deliver(results)


def solution(mesh):
    in_specs = (P("dp", None), P(None, "mp"), P("mp"), P("dp", "mp"), P(), P("mp"))
    out_specs = (P("dp", "mp"), P("dp", "mp"), P("dp", "mp"), P())
    body = fused if (mesh.shape["dp"], mesh.shape["mp"]) == (8, 4) else shards
    return jax.shard_map(body, mesh=mesh, in_specs=in_specs, out_specs=out_specs, check_vma=False)
```

```python
import functools

import jax
import jax.numpy as jnp
from jax import lax
from jax.experimental import pallas as pl
from jax.experimental.pallas import tpu as pltpu
from jax.sharding import PartitionSpec as P

COUT = 1536
K = 3072
F32 = jnp.float32
BF16 = jnp.bfloat16
MESH = pl.DeviceIdType.MESH


def shards(patches, weight, conv_bias, cotangent, row_scale, col_scale):
    output = (jnp.dot(patches, weight, preferred_element_type=jnp.float32) + conv_bias).astype(
        jnp.bfloat16
    )
    inner_width = patches.shape[1]
    strip_rows = inner_width // lax.axis_size("dp")
    local_grad = lax.dot_general(
        patches, cotangent, (((0,), (0,)), ((), ())), preferred_element_type=jnp.float32
    )
    weighted = local_grad * row_scale[:, None] * col_scale[None, :]
    small_sum = jnp.sum(weighted * weighted)
    column = lax.psum(local_grad, "dp")
    rows_here = lax.dynamic_slice_in_dim(column, lax.axis_index("dp") * strip_rows, strip_rows, 0)
    left_part = lax.dot_general(
        rows_here,
        column,
        (((1,), (1,)), ((), ())),
        precision=lax.Precision.HIGHEST,
        preferred_element_type=jnp.float32,
    )
    left_factor = lax.psum_scatter(left_part / COUT, "mp", scatter_dimension=1, tiled=True)
    full_strip = lax.all_gather(rows_here, "mp", axis=1, tiled=True)
    right_factor = lax.psum_scatter(
        lax.dot_general(
            full_strip,
            rows_here,
            (((0,), (0,)), ((), ())),
            precision=lax.Precision.HIGHEST,
            preferred_element_type=jnp.float32,
        )
        / K,
        "dp",
        scatter_dimension=0,
        tiled=True,
    )
    row_part = lax.dynamic_slice_in_dim(row_scale, lax.axis_index("dp") * strip_rows, strip_rows, 0)
    scaled_rows = rows_here * row_part[:, None] * col_scale[None, :]
    large_sum = jnp.sum(scaled_rows * scaled_rows)
    small_total, large_total = lax.psum((small_sum, large_sum), ("dp", "mp"))
    norm_pair = jnp.stack([small_total, large_total]) / (K * COUT)
    return (output, left_factor, right_factor, norm_pair)


def flip(bit, by):
    return 1 - bit if by else bit


def halves(value):
    high = value.astype(BF16)
    return high, (value - high.astype(F32)).astype(BF16)


def dot3(a, b, dims):
    a_high, a_low = a
    b_high, b_low = b
    dot = functools.partial(
        lax.dot_general, dimension_numbers=(dims, ((), ())), preferred_element_type=F32
    )
    return dot(a_high, b_high) + (dot(a_high, b_low) + dot(a_low, b_high))


GROUPS = (128, 128, 128)
LEVELS = (2, 3)
OUTER = (
    (1, 0, 3), (0, 1, 3), (0, 1, 2), (0, 1, 0), (0, 1, 1), (0, 2, 2), (0, 2, 3), (12, 0), (12, 1), (12, 2),
    (12, 3), (14, 0), (1, 0, 2), (13, 0), (0, 2, 1), (14, 1), (0, 2, 0), (1, 0, 1), (13, 1), (1, 0, 0),
    (13, 2), (1, 1, 3), (1, 1, 2), (1, 1, 0), (4, 0, 1), (4, 0, 0), (3, 0), (6, 0, 0), (1, 1, 1), (4, 0, 2),
    (6, 0, 2), (1, 2, 2), (6, 0, 1), (1, 2, 3), (4, 1, 0), (3, 1), (4, 0, 3), (9, 0, 0, 0), (6, 0, 3),
    (10, 0, 0, 0), (1, 2, 1), (1, 2, 0), (4, 1, 1), (6, 1, 1), (9, 0, 0, 1), (4, 1, 3), (9, 0, 0, 3),
    (6, 1, 3), (7, 0, 3), (5, 0), (4, 1, 2), (9, 0, 0, 2), (6, 1, 2), (5, 1), (9, 1, 0, 2), (10, 0, 0, 2),
    (9, 1, 0, 0), (10, 1, 0, 2), (7, 0, 1), (10, 1, 0, 0), (4, 2, 0), (3, 2), (10, 0, 0, 1), (9, 1, 0, 3),
    (9, 1, 0, 1), (6, 1, 0), (9, 0, 1, 0), (4, 2, 1), (9, 0, 1, 1), (6, 2, 0), (7, 1, 0), (6, 2, 1),
    (10, 1, 0, 1), (5, 2), (9, 1, 1, 0), (7, 0, 0), (10, 1, 0, 3), (7, 1, 1), (10, 0, 0, 3), (10, 0, 1, 1),
    (14, 2), (4, 2, 3), (9, 0, 1, 3), (10, 0, 1, 3), (6, 2, 3), (11, 1, 0), (9, 1, 1, 1), (7, 0, 2),
    (10, 1, 1, 1), (7, 1, 3), (9, 1, 1, 3), (10, 1, 1, 3), (4, 2, 2), (9, 0, 1, 2), (6, 2, 2), (7, 1, 2),
    (8,), (9, 1, 1, 2), (10, 1, 1, 0), (10, 0, 1, 0), (10, 1, 1, 2), (14, 3), (11, 0, 0), (10, 0, 1, 2),
    (11, 1, 1), (14, 4), (11, 0, 1), (15,),
)
INNER = (
    (0, 1, 0), (0, 1, 3), (0, 1, 2), (0, 1, 1), (12, 0), (0, 2, 3), (0, 2, 2), (12, 1), (0, 2, 1), (12, 2),
    (13, 0), (1, 0, 3), (12, 3), (1, 0, 2), (2, 0, 0), (3, 0), (2, 0, 1), (6, 0, 1), (1, 1, 3), (4, 0, 2),
    (6, 0, 2), (4, 0, 3), (1, 1, 2), (6, 0, 3), (2, 1, 1), (6, 1, 1), (2, 1, 0), (3, 1), (9, 0, 0, 0),
    (9, 0, 0, 1), (1, 2, 2), (4, 1, 3), (9, 0, 0, 3), (10, 0, 0, 0), (0, 2, 0), (6, 0, 0), (10, 0, 0, 3),
    (10, 0, 0, 1), (4, 1, 2), (9, 0, 0, 2), (5, 0), (1, 2, 3), (6, 1, 0), (7, 0, 0), (6, 1, 2), (5, 1),
    (9, 1, 0, 0), (9, 1, 0, 1), (2, 2, 1), (9, 1, 0, 2), (9, 1, 0, 3), (10, 0, 0, 2), (11, 0, 0), (2, 2, 0),
    (3, 2), (9, 0, 1, 1), (10, 1, 0, 1), (14, 0), (6, 2, 1), (9, 0, 1, 0), (7, 0, 2), (6, 2, 0),
    (10, 1, 0, 3), (14, 1), (14, 2), (10, 1, 0, 0), (5, 2), (9, 1, 1, 0), (10, 1, 1, 0), (4, 2, 3),
    (9, 1, 1, 3), (10, 0, 1, 0), (10, 1, 0, 2), (10, 1, 1, 3), (7, 1, 0), (9, 0, 1, 3), (9, 1, 1, 1),
    (4, 2, 2), (9, 1, 1, 2), (9, 0, 1, 2), (11, 1, 0), (10, 1, 1, 1), (6, 2, 3), (7, 1, 3), (10, 1, 1, 2),
    (13, 1), (14, 3), (10, 0, 1, 1), (11, 1, 1), (10, 0, 1, 2), (7, 1, 1), (6, 1, 3), (7, 0, 3), (7, 0, 1),
    (6, 2, 2), (7, 1, 2), (8,), (10, 0, 1, 3), (13, 2), (14, 4), (11, 0, 1), (15,),
)

def bounds():
    at = [0]
    for rows in GROUPS:
        at.append(at[-1] + rows)
    return at


def spans_of():
    at = bounds()
    edges = [0] + [at[n] for n in LEVELS]
    spans, levels = [], []
    for low, high in zip(edges[:-1], edges[1:]):
        level = [len(spans)]
        spans.append(((low, high - low), (0, high)))
        if low:
            level.append(len(spans))
            spans.append(((0, low), (low, high - low)))
        levels.append(level)
    return spans, levels


def kernel(
    patches_in, weight_in, bias_in, cot, row_scale, col_scale, output_out, left, right, norms, *scratch
):
    (
        grad, got_x, got_p, got_i, column, other, csplit, osplit, bcol, racc, rgot, nown, ngot,
        s_x, r_x, s_p, r_p, s_i, r_i, s_o, r_o, s_gp, s_gi, r_g,
        s_lc, r_lc, s_ly, r_ly, s_v, r_v, s_b1, s_b2, r_b, s_r, r_r, s_n, r_n,
        patches, weight, output, load, w_load, o_store,
    ) = scratch[:43]
    spans, levels = spans_of()
    edges = [0] + [bounds()[n] for n in LEVELS]
    count = len(spans)
    parts, cores, over_y = (scratch[43 + i * count:43 + (i + 1) * count] for i in range(3))
    d, m = lax.axis_index("dp"), lax.axis_index("mp")
    x, z = d % 2, d // 2
    z0, z1 = z % 2, z // 2
    c, y = m % 2, m // 2
    zs = (z, z + 1 - 2 * z0, 2 - z1, 3 - 3 * z1)
    px = (d + 1 - 2 * x, m)
    pz = (zs[1] * 2 + x, m)
    pi = ((3 - z) * 2 + x, m)
    pc = (d, m + 1 - 2 * c)
    py = (d, m + 2 - 4 * y)
    inner = (z0 + z1) % 2 == 1
    outer = (z0 + z1) % 2 == 0
    source = m == z
    relay = py[1] == z
    size = rgot.shape[1]
    half = rgot.shape[0]
    at = bounds()
    H = len(GROUPS)
    groups = [pl.ds(at[h], GROUPS[h]) for h in range(H)]

    def strip_at(k, opposite):
        return zs[k] * 2 + (1 - x if opposite else x)

    def strip(k, opposite):
        return pl.ds(pl.multiple_of(strip_at(k, opposite) * size, size), size)

    def strip_group(k, opposite, h):
        first = pl.multiple_of(strip_at(k, opposite) * size + at[h], 32)
        return pl.ds(first, GROUPS[h])

    def copy(src, dst, send, recv, to):
        return pltpu.make_async_remote_copy(
            src_ref=src, dst_ref=dst, send_sem=send, recv_sem=recv, device_id=to, device_id_type=MESH
        )

    barrier = pltpu.get_barrier_semaphore()
    for to in (px, pz, pi, pc, py):
        pl.semaphore_signal(barrier, inc=1, device_id=to, device_id_type=MESH)
    FAR = (3, 2, 1, 0)
    for o in (1, 0):
        for k in FAR:
            rows = strip(k, o)
            pltpu.make_async_copy(
                patches_in.at[:, rows], patches.at[:, rows], load.at[2 * k + o]
            ).start()
    weight_load = pltpu.make_async_copy(weight_in, weight, w_load)
    weight_load.start()
    out_copy = pltpu.make_async_copy(output, output_out, o_store)
    nown[...] = jnp.zeros_like(nown)
    racc[...] = jnp.zeros_like(racc)
    pl.semaphore_wait(barrier, 5)
    bias = bias_in[...].reshape(1, size)
    col_row = col_scale[...].reshape(1, size)
    col_square = col_row * col_row

    def folded(value, index):
        square = value * value * col_square
        total = jnp.zeros((1, size), F32)
        for b in range(size // 128):
            scale = row_scale[pl.ds(index * (size // 128) + b, 1), :]
            total += dot3(
                halves(scale * scale), halves(square[b * 128:(b + 1) * 128]), ((1,), (0,))
            )
        return total

    def col(k, h):
        return column.at[zs[k], groups[h]]

    hk = [(h, k) for h in range(H) for k in range(4)]
    xc = {
        (h, k): copy(
            grad.at[strip_group(k, 1, h)], got_x.at[k, groups[h]], s_x.at[4 * h + k], r_x.at[4 * h + k], px
        )
        for h, k in hk
    }
    swap = (1, 0, 2, 3)
    to_p = {
        (h, k): copy(
            got_x.at[k, groups[h]], got_p.at[swap[k], groups[h]],
            s_p.at[4 * h + k], r_p.at[4 * h + swap[k]], pz,
        )
        for h, k in hk
    }
    p_in = {(h, k): to_p[h, swap[k]] for h, k in hk}
    to_i = {
        (h, k): copy(
            got_x.at[k, groups[h]], got_i.at[k - 2, groups[h]],
            s_i.at[2 * h + k - 2], r_i.at[2 * h + k - 2], pi,
        )
        for h, k in hk if k >= 2
    }

    def pass_on(k, h, index, send, to):
        return copy(col(k, h), col(k, h), send, r_g.at[4 * h + index], to)

    gp = {(h, k): pass_on(k, h, swap[k], s_gp.at[4 * h + k], pz) for h, k in hk}
    gi = {
        (h, k): pass_on(k, h, k + 2, s_gi.at[2 * h + k], pi) for h in range(H) for k in range(2)
    }
    g_in = {(h, k): pass_on(k, h, k, s_gp.at[0], pz) for h, k in hk}
    o_copy = [copy(col(0, h), other.at[groups[h]], s_o.at[h], r_o.at[h], px) for h in range(H)]

    def b_copy(src, h, k, send, to):
        return copy(src, bcol.at[k, groups[h]], send.at[4 * h + k], r_b.at[4 * h + k], to)

    b_core = {(h, k): b_copy(col(k, h), h, k, s_b1, pc) for h, k in hk}
    b_y = {(h, k): b_copy(col(k, h), h, k, s_b2, py) for h, k in hk}
    b_on = {(h, k): b_copy(bcol.at[k, groups[h]], h, k, s_b1, pc) for h, k in hk}
    wpk = [(w, p, k) for w in range(2) for p in range(count) for k in range(4)]
    lcc = {
        (w, p, k): copy(
            parts[p].at[w, k], cores[p].at[w, k],
            s_lc.at[(w * count + p) * 4 + k], r_lc.at[(w * count + p) * 4 + k], pc,
        )
        for w, p, k in wpk
    }
    lyc = {
        (w, p, k): copy(
            parts[p].at[w, k], over_y[p].at[w], s_ly.at[w * count + p], r_ly.at[w * count + p], py
        )
        for w, p, k in wpk
    }
    at_k = 0
    for k in range(1, 4):
        at_k = at_k + k * (zs[k] == m).astype(jnp.int32)
    left_at = pl.multiple_of(x * size, size)

    def place(p):
        (row, rows), (first, cols) = spans[p]
        return left.at[pl.ds(row, rows), pl.ds(pl.multiple_of(left_at + first, 128), cols)]

    vc = [copy(over_y[p].at[1], place(p), s_v.at[p], r_v.at[p], px) for p in range(count)]
    rc = copy(racc.at[pl.ds(pl.multiple_of((1 - x) * half, half), half)], rgot, s_r, r_r, px)
    n_to = (pc, pz, pi, py, px)
    nc = [copy(nown.at[i], ngot.at[i], s_n.at[i], r_n.at[i], n_to[i]) for i in range(5)]

    def split(value, ref, g):
        high, low = halves(value)
        ref[0, g, :] = high
        ref[1, g, :] = low

    def zs_dynamic(k):
        low, high = k % 2, k // 2
        near = z + low - 2 * z0 * low
        beyond = 2 - z1 + low * (1 - 2 * z1)
        return near + high * (beyond - near)

    def make_grad(i, _):
        k, opposite = 3 - i % 4, 1 - i // 4
        index = zs_dynamic(k) * 2 + x + opposite - 2 * x * opposite
        rows = pl.ds(pl.multiple_of(index * size, size), size)
        pltpu.make_async_copy(
            patches_in.at[:, rows], patches.at[:, rows], load.at[2 * k + opposite]
        ).wait()
        grad[rows, :] = lax.dot_general(
            patches[:, rows], cot[...], (((0,), (0,)), ((), ())), preferred_element_type=F32
        )

        @pl.when(opposite == 1)
        def _():
            first = pl.ds(pl.multiple_of(index * size, size), GROUPS[0])
            copy(grad.at[first], got_x.at[k, groups[0]], s_x.at[k], r_x.at[k], px).start()

        return 0

    def xs(inside, h, k):
        xc[h, k].start()

    def rs(inside, h, k):
        g = groups[h]
        xc[h, k].wait_recv()
        value = got_x[k, g, :] + grad[strip_group(k, 0, h), :]
        if inside:
            p_in[h, k].wait_recv()
            value += got_p[k, g, :]
        got_x[k, g, :] = value
        (to_i if inside else to_p)[h, k].start()

    def fn(inside, h, k):
        g = groups[h]
        xc[h, k].wait_recv()
        p_in[h, k].wait_recv()
        to_i[h, k + 2].wait_recv()
        value = got_x[k, g, :] + grad[strip_group(k, 0, h), :] + got_p[k, g, :] + got_i[k, g, :]
        column[zs[k], g, :] = value
        gp[h, k].start()
        gi[h, k].start()
        split(value, csplit.at[:, k], g)

    def os(inside, h):
        o_copy[h].start()

    def ar(inside, h, k):
        g_in[h, k].wait_recv()
        if inside:
            gp[h, k].start()
        split(column[zs[k], groups[h], :], csplit.at[:, k], groups[h])

    def oth(inside, h):
        o_copy[h].wait_recv()
        split(other[groups[h], :], osplit, groups[h])

    def bs(inside, h, k):
        @pl.when(source)
        def _():
            b_y[h, k].start()
            b_core[h, k].start()
            bcol[k, groups[h], :] = column[zs[k], groups[h], :]

        @pl.when(jnp.logical_not(source))
        def _():
            b_core[h, k].wait_recv()

        @pl.when(relay)
        def _():
            b_on[h, k].start()

    def rt(inside, level, k):
        g = pl.ds(edges[level], edges[level + 1] - edges[level])
        racc[...] += dot3(
            halves(bcol[k, g, :]), (csplit[0, k, g, :], csplit[1, k, g, :]), ((0,), (0,))
        )

    def start_rc(inside):
        rc.start()

    def lu(inside, w, level, k):
        mine = osplit if w else csplit.at[:, 0]
        for p in levels[level]:
            (row, rows), (first, cols) = spans[p]
            g, f = pl.ds(row, rows), pl.ds(first, cols)
            parts[p][w, k] = dot3(
                (mine[0, g, :], mine[1, g, :]), (csplit[0, k, f, :], csplit[1, k, f, :]), ((1,), (1,))
            )

        @pl.when(zs[k] % 2 != c)
        def _():
            for p in levels[level]:
                lcc[w, p, k].start()

    def rd(inside, w, level, k):
        @pl.when(zs[k] % 2 == c)
        def _():
            for p in levels[level]:
                lcc[w, p, k].wait_recv()
                parts[p][w, k] += cores[p][w, k]

            @pl.when(zs[k] // 2 != y)
            def _():
                for p in levels[level]:
                    lyc[w, p, k].start()

    def fi(inside, w, level):
        for p in levels[level]:
            lyc[w, p, 0].wait_recv()
            total = (parts[p][w, at_k] + over_y[p][w]) * (1.0 / COUT)
            if w:
                over_y[p][1] = total
                vc[p].start()
            else:
                place(p)[...] = total

    def small_step(s, _):
        rows = pl.ds(pl.multiple_of(s * size, size), size)
        nown[0, 0:1, :] += folded(grad[rows, :], s)
        return 0

    def small(inside, i):
        lax.fori_loop(2 * i, 2 * i + 2, small_step, 0)

    def out_step(i, _):
        rows = pl.ds(pl.multiple_of(i * 128, 128), 128)
        value = jnp.dot(patches[rows, :], weight[...], preferred_element_type=F32) + bias
        output[rows, :] = value.astype(BF16)
        return 0

    tiles = patches.shape[0] // 128
    cuts = (0, tiles // 3, 2 * (tiles // 3), tiles)

    def out(inside, i):
        if i == 0:
            weight_load.wait()
        lax.fori_loop(cuts[i], cuts[i + 1], out_step, 0)
        if i == 2:
            out_copy.start()

    def nm(inside, i):
        if i == 0:
            if inside:
                nown[0, 8:9, :] = folded(column[z], strip_at(0, 0)) + folded(
                    column[zs[1]], strip_at(1, 0)
                )
        else:
            nc[i - 1].wait_recv()
            nown[i] = nown[i - 1] + ngot[i - 1]
        nc[i].start()

    def finish(inside):
        nc[4].wait_recv()
        both = nown[4] + ngot[4]
        norms[0] = jnp.sum(both[0:8]) / (K * COUT)
        norms[1] = jnp.sum(both[8:16]) / (K * COUT)
        rc.wait_recv()
        right[...] = (racc[pl.ds(pl.multiple_of(x * half, half), half), :] + rgot[...]) * (1.0 / K)
        for one in vc:
            one.wait_recv()
        out_copy.wait()

    lax.fori_loop(0, 8, make_grad, 0)
    steps = (xs, rs, fn, os, ar, oth, bs, rt, start_rc, lu, rd, fi, small, out, nm, finish)

    @pl.when(outer)
    def _():
        for code, *where in OUTER:
            steps[code](False, *where)

    @pl.when(inner)
    def _():
        for code, *where in INNER:
            steps[code](True, *where)

    sent = [*xc.values(), *o_copy, *vc, rc, *nc]
    for w in range(2):
        for p in range(count):
            sent.append(lyc[w, p, 0])
    for one in sent:
        one.wait_send()

    @pl.when(outer)
    def _():
        for key in hk:
            to_p[key].wait_send()

    @pl.when(inner)
    def _():
        for one in (*to_i.values(), *gp.values(), *gi.values()):
            one.wait_send()

    @pl.when(source)
    def _():
        for key in hk:
            b_y[key].wait_send()
            b_core[key].wait_send()

    @pl.when(relay)
    def _():
        for key in hk:
            b_on[key].wait_send()

    for k in range(4):

        @pl.when(zs[k] % 2 != c)
        def _():
            for w in range(2):
                for p in range(count):
                    lcc[w, p, k].wait_send()


def deliver_kernel(output_in, left_in, right_in, norms_in, output, left, right, norms, sems):
    norms[0] = norms_in[0]
    norms[1] = norms_in[1]
    pairs = ((output_in, output), (left_in, left), (right_in, right))
    copies = [pltpu.make_async_copy(a, b, sems.at[i]) for i, (a, b) in enumerate(pairs)]
    for one in copies:
        one.start()
    for one in copies:
        one.wait()


def deliver(results):
    vmem = pl.BlockSpec(memory_space=pltpu.VMEM)
    hbm = pl.BlockSpec(memory_space=pl.ANY)
    smem = pl.BlockSpec(memory_space=pltpu.SMEM)
    return pl.pallas_call(
        deliver_kernel,
        out_shape=tuple(jax.ShapeDtypeStruct(r.shape, r.dtype) for r in results),
        in_specs=[vmem, vmem, vmem, smem],
        out_specs=(hbm, hbm, hbm, smem),
        scratch_shapes=[pltpu.SemaphoreType.DMA((3,))],
    )(*results)


def fused(patches, weight, conv_bias, cotangent, row_scale, col_scale):
    rows, width = patches.shape
    cols = cotangent.shape[1]
    size = width // 8
    H = len(GROUPS)
    vmem = pl.BlockSpec(memory_space=pltpu.VMEM)
    hbm = pl.BlockSpec(memory_space=pl.ANY)
    dma = pltpu.SemaphoreType.DMA
    one = dma
    spans, _ = spans_of()
    count = len(spans)
    shapes = [(a[1], b[1]) for a, b in spans]
    results = pl.pallas_call(
        kernel,
        out_shape=(
            jax.ShapeDtypeStruct((rows, cols), BF16),
            jax.ShapeDtypeStruct((size, width // 4), F32),
            jax.ShapeDtypeStruct((cols // 2, cols), F32),
            jax.ShapeDtypeStruct((2,), F32),
        ),
        in_specs=[hbm, hbm, vmem, vmem, vmem, vmem],
        out_specs=(hbm, vmem, vmem, pl.BlockSpec(memory_space=pltpu.SMEM)),
        scratch_shapes=[
            pltpu.VMEM((width, cols), F32),
            pltpu.VMEM((4, size, cols), F32),
            pltpu.VMEM((4, size, cols), F32),
            pltpu.VMEM((2, size, cols), F32),
            pltpu.VMEM((4, size, cols), F32),
            pltpu.VMEM((size, cols), F32),
            pltpu.VMEM((2, 4, size, cols), BF16),
            pltpu.VMEM((2, size, cols), BF16),
            pltpu.VMEM((4, size, cols), F32),
            pltpu.VMEM((cols, cols), F32),
            pltpu.VMEM((cols // 2, cols), F32),
            pltpu.VMEM((5, 16, cols), F32),
            pltpu.VMEM((5, 16, cols), F32),
            dma((4 * H,)), dma((4 * H,)), dma((4 * H,)), dma((4 * H,)), dma((2 * H,)), dma((2 * H,)),
            dma((H,)), dma((H,)), dma((4 * H,)), dma((2 * H,)), dma((4 * H,)),
            dma((8 * count,)), dma((8 * count,)), dma((2 * count,)), dma((2 * count,)),
            dma((count,)), dma((count,)),
            dma((4 * H,)), dma((4 * H,)), dma((4 * H,)), one, one,
            dma((5,)), dma((5,)),
            pltpu.VMEM((rows, width), BF16),
            pltpu.VMEM((width, cols), BF16),
            pltpu.VMEM((rows, cols), BF16),
            dma((8,)), one, one,
            *[pltpu.VMEM((2, 4, *shape), F32) for shape in shapes],
            *[pltpu.VMEM((2, 4, *shape), F32) for shape in shapes],
            *[pltpu.VMEM((2, *shape), F32) for shape in shapes],
        ],
        compiler_params=pltpu.CompilerParams(
            collective_id=0, has_side_effects=True, vmem_limit_bytes=61 * 1024 * 1024
        ),
    )(
        patches, weight, conv_bias, cotangent, row_scale.reshape(-1, 128), col_scale
    )
    return deliver(results)


def solution(mesh):
    in_specs = (P("dp", None), P(None, "mp"), P("mp"), P("dp", "mp"), P(), P("mp"))
    out_specs = (P("dp", "mp"), P("dp", "mp"), P("dp", "mp"), P())
    body = fused if (mesh.shape["dp"], mesh.shape["mp"]) == (8, 4) else shards
    return jax.shard_map(body, mesh=mesh, in_specs=in_specs, out_specs=out_specs, check_vma=False)
```

```python
import functools

import jax
import jax.numpy as jnp
from jax import lax
from jax.experimental import pallas as pl
from jax.experimental.pallas import tpu as pltpu
from jax.sharding import PartitionSpec as P

COUT = 1536
K = 3072
F32 = jnp.float32
BF16 = jnp.bfloat16
MESH = pl.DeviceIdType.MESH


def shards(patches, weight, conv_bias, cotangent, row_scale, col_scale):
    output = (jnp.dot(patches, weight, preferred_element_type=jnp.float32) + conv_bias).astype(
        jnp.bfloat16
    )
    inner_width = patches.shape[1]
    strip_rows = inner_width // lax.axis_size("dp")
    local_grad = lax.dot_general(
        patches, cotangent, (((0,), (0,)), ((), ())), preferred_element_type=jnp.float32
    )
    weighted = local_grad * row_scale[:, None] * col_scale[None, :]
    small_sum = jnp.sum(weighted * weighted)
    column = lax.psum(local_grad, "dp")
    rows_here = lax.dynamic_slice_in_dim(column, lax.axis_index("dp") * strip_rows, strip_rows, 0)
    left_part = lax.dot_general(
        rows_here,
        column,
        (((1,), (1,)), ((), ())),
        precision=lax.Precision.HIGHEST,
        preferred_element_type=jnp.float32,
    )
    left_factor = lax.psum_scatter(left_part / COUT, "mp", scatter_dimension=1, tiled=True)
    full_strip = lax.all_gather(rows_here, "mp", axis=1, tiled=True)
    right_factor = lax.psum_scatter(
        lax.dot_general(
            full_strip,
            rows_here,
            (((0,), (0,)), ((), ())),
            precision=lax.Precision.HIGHEST,
            preferred_element_type=jnp.float32,
        )
        / K,
        "dp",
        scatter_dimension=0,
        tiled=True,
    )
    row_part = lax.dynamic_slice_in_dim(row_scale, lax.axis_index("dp") * strip_rows, strip_rows, 0)
    scaled_rows = rows_here * row_part[:, None] * col_scale[None, :]
    large_sum = jnp.sum(scaled_rows * scaled_rows)
    small_total, large_total = lax.psum((small_sum, large_sum), ("dp", "mp"))
    norm_pair = jnp.stack([small_total, large_total]) / (K * COUT)
    return (output, left_factor, right_factor, norm_pair)


def flip(bit, by):
    return 1 - bit if by else bit


def halves(value):
    high = value.astype(BF16)
    return high, (value - high.astype(F32)).astype(BF16)


def dot3(a, b, dims):
    a_high, a_low = a
    b_high, b_low = b
    dot = functools.partial(
        lax.dot_general, dimension_numbers=(dims, ((), ())), preferred_element_type=F32
    )
    return dot(a_high, b_high) + (dot(a_high, b_low) + dot(a_low, b_high))


GROUPS = (128, 128, 128)
LEVELS = (2, 3)
OUTER = (
    (1, 0, 3), (0, 1, 3), (0, 1, 2), (0, 1, 0), (0, 1, 1), (12, 0), (12, 1), (0, 2, 2), (0, 2, 3), (0, 2, 0),
    (12, 2), (12, 3), (0, 2, 1), (1, 0, 2), (13, 0), (1, 0, 1), (13, 1), (1, 0, 0), (1, 1, 3), (14, 0),
    (1, 1, 2), (1, 1, 0), (4, 0, 0), (4, 0, 1), (1, 1, 1), (4, 0, 2), (6, 0, 1), (1, 2, 2), (4, 0, 3),
    (6, 0, 0), (1, 2, 3), (14, 1), (4, 1, 0), (3, 1), (6, 1, 0), (7, 0, 0), (9, 0, 0, 0), (6, 0, 2),
    (1, 2, 0), (6, 0, 3), (4, 1, 1), (9, 0, 0, 1), (10, 0, 0, 0), (6, 1, 1), (1, 2, 1), (4, 1, 3), (6, 1, 3),
    (7, 0, 3), (3, 0), (9, 0, 0, 3), (10, 0, 0, 3), (7, 0, 1), (4, 1, 2), (6, 1, 2), (9, 0, 0, 2),
    (10, 0, 0, 1), (5, 1), (5, 0), (9, 1, 0, 0), (9, 1, 0, 2), (9, 1, 0, 3), (7, 0, 2), (4, 2, 0), (3, 2),
    (6, 2, 0), (10, 1, 0, 0), (9, 0, 1, 0), (9, 1, 0, 1), (7, 1, 0), (10, 1, 0, 1), (4, 2, 1), (6, 2, 1),
    (9, 0, 1, 1), (10, 1, 0, 3), (10, 1, 0, 2), (5, 2), (9, 1, 1, 1), (7, 1, 1), (9, 1, 1, 0), (14, 2),
    (10, 1, 1, 1), (4, 2, 3), (9, 1, 1, 3), (11, 1, 0), (10, 1, 1, 0), (6, 2, 3), (7, 1, 3), (4, 2, 2),
    (6, 2, 2), (7, 1, 2), (8,), (10, 1, 1, 3), (9, 1, 1, 2), (10, 0, 0, 2), (10, 0, 1, 1), (10, 1, 1, 2),
    (9, 0, 1, 2), (14, 3), (10, 0, 1, 0), (10, 0, 1, 2), (9, 0, 1, 3), (11, 1, 1), (10, 0, 1, 3), (11, 0, 0),
    (14, 4), (13, 2), (11, 0, 1), (15,),
)
INNER = (
    (0, 2, 3), (0, 1, 3), (12, 0), (12, 1), (13, 0), (0, 1, 2), (1, 0, 3), (12, 2), (0, 1, 1), (13, 1),
    (1, 0, 2), (13, 2), (2, 0, 0), (0, 1, 0), (0, 2, 2), (2, 0, 1), (1, 1, 3), (4, 0, 2), (6, 0, 2),
    (1, 1, 2), (4, 0, 3), (6, 0, 3), (2, 1, 1), (6, 1, 1), (2, 1, 0), (3, 1), (3, 0), (9, 0, 0, 1),
    (9, 0, 0, 0), (4, 1, 3), (9, 0, 0, 3), (10, 0, 0, 3), (1, 2, 2), (0, 2, 1), (12, 3), (10, 0, 0, 1),
    (4, 1, 2), (1, 2, 3), (5, 1), (9, 0, 0, 2), (10, 0, 0, 2), (6, 1, 3), (10, 0, 0, 0), (5, 0), (9, 1, 0, 0),
    (9, 1, 0, 2), (0, 2, 0), (10, 1, 0, 2), (9, 1, 0, 1), (2, 2, 1), (9, 1, 0, 3), (7, 0, 3), (10, 1, 0, 0),
    (6, 0, 1), (10, 1, 0, 1), (2, 2, 0), (3, 2), (6, 2, 0), (14, 0), (7, 1, 0), (9, 0, 1, 1), (6, 1, 2),
    (14, 1), (14, 2), (11, 0, 0), (4, 2, 3), (10, 0, 1, 1), (6, 2, 1), (10, 1, 0, 3), (5, 2), (9, 1, 1, 3),
    (9, 1, 1, 1), (9, 1, 1, 0), (7, 1, 1), (4, 2, 2), (6, 2, 3), (7, 1, 3), (10, 1, 1, 1), (11, 1, 0),
    (6, 0, 0), (7, 0, 1), (7, 0, 2), (9, 0, 1, 2), (6, 2, 2), (7, 1, 2), (6, 1, 0), (7, 0, 0), (8,),
    (9, 1, 1, 2), (10, 1, 1, 3), (10, 1, 1, 0), (9, 0, 1, 0), (10, 1, 1, 2), (14, 3), (10, 0, 1, 2),
    (9, 0, 1, 3), (10, 0, 1, 3), (11, 1, 1), (14, 4), (10, 0, 1, 0), (11, 0, 1), (15,),
)

def bounds():
    at = [0]
    for rows in GROUPS:
        at.append(at[-1] + rows)
    return at


def spans_of():
    at = bounds()
    edges = [0] + [at[n] for n in LEVELS]
    spans, levels = [], []
    for low, high in zip(edges[:-1], edges[1:]):
        level = [len(spans)]
        spans.append(((low, high - low), (0, high)))
        if low:
            level.append(len(spans))
            spans.append(((0, low), (low, high - low)))
        levels.append(level)
    return spans, levels


def kernel(
    patches_in, weight_in, bias_in, cot, row_scale, col_scale, output_out, left, right, norms, *scratch
):
    (
        grad, got_x, got_p, got_i, column, other, csplit, osplit, bcol, racc, rgot, nown, ngot,
        s_x, r_x, s_p, r_p, s_i, r_i, s_o, r_o, s_gp, s_gi, r_g,
        s_lc, r_lc, s_ly, r_ly, s_v, r_v, s_b1, s_b2, r_b, s_r, r_r, s_n, r_n,
        patches, weight, output, load, w_load, o_store,
    ) = scratch[:43]
    spans, levels = spans_of()
    edges = [0] + [bounds()[n] for n in LEVELS]
    count = len(spans)
    parts, cores, over_y = (scratch[43 + i * count:43 + (i + 1) * count] for i in range(3))
    d, m = lax.axis_index("dp"), lax.axis_index("mp")
    x, z = d % 2, d // 2
    z0, z1 = z % 2, z // 2
    c, y = m % 2, m // 2
    zs = (z, z + 1 - 2 * z0, 2 - z1, 3 - 3 * z1)
    px = (d + 1 - 2 * x, m)
    pz = (zs[1] * 2 + x, m)
    pi = ((3 - z) * 2 + x, m)
    pc = (d, m + 1 - 2 * c)
    py = (d, m + 2 - 4 * y)
    inner = (z0 + z1) % 2 == 1
    outer = (z0 + z1) % 2 == 0
    source = m == z
    relay = py[1] == z
    size = rgot.shape[1]
    half = rgot.shape[0]
    at = bounds()
    H = len(GROUPS)
    groups = [pl.ds(at[h], GROUPS[h]) for h in range(H)]

    def strip_at(k, opposite):
        return zs[k] * 2 + (1 - x if opposite else x)

    def strip(k, opposite):
        return pl.ds(pl.multiple_of(strip_at(k, opposite) * size, size), size)

    def strip_group(k, opposite, h):
        first = pl.multiple_of(strip_at(k, opposite) * size + at[h], 32)
        return pl.ds(first, GROUPS[h])

    def copy(src, dst, send, recv, to):
        return pltpu.make_async_remote_copy(
            src_ref=src, dst_ref=dst, send_sem=send, recv_sem=recv, device_id=to, device_id_type=MESH
        )

    barrier = pltpu.get_barrier_semaphore()
    for to in (px, pz, pi, pc, py):
        pl.semaphore_signal(barrier, inc=1, device_id=to, device_id_type=MESH)
    FAR = (3, 2, 1, 0)
    for o in (1, 0):
        for k in FAR:
            rows = strip(k, o)
            pltpu.make_async_copy(
                patches_in.at[:, rows], patches.at[:, rows], load.at[2 * k + o]
            ).start()
    weight_load = pltpu.make_async_copy(weight_in, weight, w_load)
    weight_load.start()
    out_copy = pltpu.make_async_copy(output, output_out, o_store)
    nown[...] = jnp.zeros_like(nown)
    racc[...] = jnp.zeros_like(racc)
    bias = bias_in[...].reshape(1, size)
    col_row = col_scale[...].reshape(1, size)
    col_square = col_row * col_row

    def folded(value, index):
        square = value * value * col_square
        total = jnp.zeros((1, size), F32)
        for b in range(size // 128):
            scale = row_scale[pl.ds(index * (size // 128) + b, 1), :]
            total += dot3(
                halves(scale * scale), halves(square[b * 128:(b + 1) * 128]), ((1,), (0,))
            )
        return total

    def col(k, h):
        return column.at[zs[k], groups[h]]

    hk = [(h, k) for h in range(H) for k in range(4)]
    xc = {
        (h, k): copy(
            grad.at[strip_group(k, 1, h)], got_x.at[k, groups[h]], s_x.at[4 * h + k], r_x.at[4 * h + k], px
        )
        for h, k in hk
    }
    swap = (1, 0, 2, 3)
    to_p = {
        (h, k): copy(
            got_x.at[k, groups[h]], got_p.at[swap[k], groups[h]],
            s_p.at[4 * h + k], r_p.at[4 * h + swap[k]], pz,
        )
        for h, k in hk
    }
    p_in = {(h, k): to_p[h, swap[k]] for h, k in hk}
    to_i = {
        (h, k): copy(
            got_x.at[k, groups[h]], got_i.at[k - 2, groups[h]],
            s_i.at[2 * h + k - 2], r_i.at[2 * h + k - 2], pi,
        )
        for h, k in hk if k >= 2
    }

    def pass_on(k, h, index, send, to):
        return copy(col(k, h), col(k, h), send, r_g.at[4 * h + index], to)

    gp = {(h, k): pass_on(k, h, swap[k], s_gp.at[4 * h + k], pz) for h, k in hk}
    gi = {
        (h, k): pass_on(k, h, k + 2, s_gi.at[2 * h + k], pi) for h in range(H) for k in range(2)
    }
    g_in = {(h, k): pass_on(k, h, k, s_gp.at[0], pz) for h, k in hk}
    o_copy = [copy(col(0, h), other.at[groups[h]], s_o.at[h], r_o.at[h], px) for h in range(H)]

    def b_copy(src, h, k, send, to):
        return copy(src, bcol.at[k, groups[h]], send.at[4 * h + k], r_b.at[4 * h + k], to)

    b_core = {(h, k): b_copy(col(k, h), h, k, s_b1, pc) for h, k in hk}
    b_y = {(h, k): b_copy(col(k, h), h, k, s_b2, py) for h, k in hk}
    b_on = {(h, k): b_copy(bcol.at[k, groups[h]], h, k, s_b1, pc) for h, k in hk}
    wpk = [(w, p, k) for w in range(2) for p in range(count) for k in range(4)]
    lcc = {
        (w, p, k): copy(
            parts[p].at[w, k], cores[p].at[w, k],
            s_lc.at[(w * count + p) * 4 + k], r_lc.at[(w * count + p) * 4 + k], pc,
        )
        for w, p, k in wpk
    }
    lyc = {
        (w, p, k): copy(
            parts[p].at[w, k], over_y[p].at[w], s_ly.at[w * count + p], r_ly.at[w * count + p], py
        )
        for w, p, k in wpk
    }
    at_k = 0
    for k in range(1, 4):
        at_k = at_k + k * (zs[k] == m).astype(jnp.int32)
    left_at = pl.multiple_of(x * size, size)

    def place(p):
        (row, rows), (first, cols) = spans[p]
        return left.at[pl.ds(row, rows), pl.ds(pl.multiple_of(left_at + first, 128), cols)]

    vc = [copy(over_y[p].at[1], place(p), s_v.at[p], r_v.at[p], px) for p in range(count)]
    rc = copy(racc.at[pl.ds(pl.multiple_of((1 - x) * half, half), half)], rgot, s_r, r_r, px)
    n_to = (pc, pz, pi, py, px)
    nc = [copy(nown.at[i], ngot.at[i], s_n.at[i], r_n.at[i], n_to[i]) for i in range(5)]

    def split(value, ref, g):
        high, low = halves(value)
        ref[0, g, :] = high
        ref[1, g, :] = low

    def zs_dynamic(k):
        low, high = k % 2, k // 2
        near = z + low - 2 * z0 * low
        beyond = 2 - z1 + low * (1 - 2 * z1)
        return near + high * (beyond - near)

    def make_grad(i, _):
        k, opposite = 3 - i % 4, 1 - i // 4
        index = zs_dynamic(k) * 2 + x + opposite - 2 * x * opposite
        rows = pl.ds(pl.multiple_of(index * size, size), size)
        pltpu.make_async_copy(
            patches_in.at[:, rows], patches.at[:, rows], load.at[2 * k + opposite]
        ).wait()
        grad[rows, :] = lax.dot_general(
            patches[:, rows], cot[...], (((0,), (0,)), ((), ())), preferred_element_type=F32
        )

        @pl.when(i == 0)
        def _():
            pl.semaphore_wait(barrier, 5)

        @pl.when(opposite == 1)
        def _():
            first = pl.ds(pl.multiple_of(index * size, size), GROUPS[0])
            copy(grad.at[first], got_x.at[k, groups[0]], s_x.at[k], r_x.at[k], px).start()

        return 0

    def xs(inside, h, k):
        xc[h, k].start()

    def rs(inside, h, k):
        g = groups[h]
        xc[h, k].wait_recv()
        value = got_x[k, g, :] + grad[strip_group(k, 0, h), :]
        if inside:
            p_in[h, k].wait_recv()
            value += got_p[k, g, :]
        got_x[k, g, :] = value
        (to_i if inside else to_p)[h, k].start()

    def fn(inside, h, k):
        g = groups[h]
        xc[h, k].wait_recv()
        p_in[h, k].wait_recv()
        to_i[h, k + 2].wait_recv()
        value = got_x[k, g, :] + grad[strip_group(k, 0, h), :] + got_p[k, g, :] + got_i[k, g, :]
        column[zs[k], g, :] = value
        gp[h, k].start()
        gi[h, k].start()
        split(value, csplit.at[:, k], g)

    def os(inside, h):
        o_copy[h].start()

    def ar(inside, h, k):
        g_in[h, k].wait_recv()
        if inside:
            gp[h, k].start()
        split(column[zs[k], groups[h], :], csplit.at[:, k], groups[h])

    def oth(inside, h):
        o_copy[h].wait_recv()
        split(other[groups[h], :], osplit, groups[h])

    def bs(inside, h, k):
        @pl.when(source)
        def _():
            b_y[h, k].start()
            b_core[h, k].start()
            bcol[k, groups[h], :] = column[zs[k], groups[h], :]

        @pl.when(jnp.logical_not(source))
        def _():
            b_core[h, k].wait_recv()

        @pl.when(relay)
        def _():
            b_on[h, k].start()

    def rt(inside, level, k):
        g = pl.ds(edges[level], edges[level + 1] - edges[level])
        racc[...] += dot3(
            halves(bcol[k, g, :]), (csplit[0, k, g, :], csplit[1, k, g, :]), ((0,), (0,))
        )

    def start_rc(inside):
        rc.start()

    def lu(inside, w, level, k):
        mine = osplit if w else csplit.at[:, 0]
        for p in levels[level]:
            (row, rows), (first, cols) = spans[p]
            g, f = pl.ds(row, rows), pl.ds(first, cols)
            parts[p][w, k] = dot3(
                (mine[0, g, :], mine[1, g, :]), (csplit[0, k, f, :], csplit[1, k, f, :]), ((1,), (1,))
            )

        @pl.when(zs[k] % 2 != c)
        def _():
            for p in levels[level]:
                lcc[w, p, k].start()

    def rd(inside, w, level, k):
        @pl.when(zs[k] % 2 == c)
        def _():
            for p in levels[level]:
                lcc[w, p, k].wait_recv()
                parts[p][w, k] += cores[p][w, k]

            @pl.when(zs[k] // 2 != y)
            def _():
                for p in levels[level]:
                    lyc[w, p, k].start()

    def fi(inside, w, level):
        for p in levels[level]:
            lyc[w, p, 0].wait_recv()
            total = (parts[p][w, at_k] + over_y[p][w]) * (1.0 / COUT)
            if w:
                over_y[p][1] = total
                vc[p].start()
            else:
                place(p)[...] = total

    def small_step(s, _):
        rows = pl.ds(pl.multiple_of(s * size, size), size)
        nown[0, 0:1, :] += folded(grad[rows, :], s)
        return 0

    def small(inside, i):
        lax.fori_loop(2 * i, 2 * i + 2, small_step, 0)

    def out_step(i, _):
        rows = pl.ds(pl.multiple_of(i * 128, 128), 128)
        value = jnp.dot(patches[rows, :], weight[...], preferred_element_type=F32) + bias
        output[rows, :] = value.astype(BF16)
        return 0

    tiles = patches.shape[0] // 128
    cuts = (0, tiles // 3, 2 * (tiles // 3), tiles)

    def out(inside, i):
        if i == 0:
            weight_load.wait()
        lax.fori_loop(cuts[i], cuts[i + 1], out_step, 0)
        if i == 2:
            out_copy.start()

    def nm(inside, i):
        if i == 0:
            if inside:
                nown[0, 8:9, :] = folded(column[z], strip_at(0, 0)) + folded(
                    column[zs[1]], strip_at(1, 0)
                )
        else:
            nc[i - 1].wait_recv()
            nown[i] = nown[i - 1] + ngot[i - 1]
        nc[i].start()

    def finish(inside):
        nc[4].wait_recv()
        both = nown[4] + ngot[4]
        norms[0] = jnp.sum(both[0:8]) / (K * COUT)
        norms[1] = jnp.sum(both[8:16]) / (K * COUT)
        rc.wait_recv()
        right[...] = (racc[pl.ds(pl.multiple_of(x * half, half), half), :] + rgot[...]) * (1.0 / K)
        for one in vc:
            one.wait_recv()
        out_copy.wait()

    lax.fori_loop(0, 8, make_grad, 0)
    steps = (xs, rs, fn, os, ar, oth, bs, rt, start_rc, lu, rd, fi, small, out, nm, finish)

    @pl.when(outer)
    def _():
        for code, *where in OUTER:
            steps[code](False, *where)

    @pl.when(inner)
    def _():
        for code, *where in INNER:
            steps[code](True, *where)

    sent = [*xc.values(), *o_copy, *vc, rc, *nc]
    for w in range(2):
        for p in range(count):
            sent.append(lyc[w, p, 0])
    for one in sent:
        one.wait_send()

    @pl.when(outer)
    def _():
        for key in hk:
            to_p[key].wait_send()

    @pl.when(inner)
    def _():
        for one in (*to_i.values(), *gp.values(), *gi.values()):
            one.wait_send()

    @pl.when(source)
    def _():
        for key in hk:
            b_y[key].wait_send()
            b_core[key].wait_send()

    @pl.when(relay)
    def _():
        for key in hk:
            b_on[key].wait_send()

    for k in range(4):

        @pl.when(zs[k] % 2 != c)
        def _():
            for w in range(2):
                for p in range(count):
                    lcc[w, p, k].wait_send()


def deliver_kernel(output_in, left_in, right_in, norms_in, output, left, right, norms, sems):
    norms[0] = norms_in[0]
    norms[1] = norms_in[1]
    pairs = ((output_in, output), (left_in, left), (right_in, right))
    copies = [pltpu.make_async_copy(a, b, sems.at[i]) for i, (a, b) in enumerate(pairs)]
    for one in copies:
        one.start()
    for one in copies:
        one.wait()


def deliver(results):
    vmem = pl.BlockSpec(memory_space=pltpu.VMEM)
    hbm = pl.BlockSpec(memory_space=pl.ANY)
    smem = pl.BlockSpec(memory_space=pltpu.SMEM)
    return pl.pallas_call(
        deliver_kernel,
        out_shape=tuple(jax.ShapeDtypeStruct(r.shape, r.dtype) for r in results),
        in_specs=[vmem, vmem, vmem, smem],
        out_specs=(hbm, hbm, hbm, smem),
        scratch_shapes=[pltpu.SemaphoreType.DMA((3,))],
    )(*results)


def fused(patches, weight, conv_bias, cotangent, row_scale, col_scale):
    rows, width = patches.shape
    cols = cotangent.shape[1]
    size = width // 8
    H = len(GROUPS)
    vmem = pl.BlockSpec(memory_space=pltpu.VMEM)
    hbm = pl.BlockSpec(memory_space=pl.ANY)
    dma = pltpu.SemaphoreType.DMA
    one = dma
    spans, _ = spans_of()
    count = len(spans)
    shapes = [(a[1], b[1]) for a, b in spans]
    results = pl.pallas_call(
        kernel,
        out_shape=(
            jax.ShapeDtypeStruct((rows, cols), BF16),
            jax.ShapeDtypeStruct((size, width // 4), F32),
            jax.ShapeDtypeStruct((cols // 2, cols), F32),
            jax.ShapeDtypeStruct((2,), F32),
        ),
        in_specs=[hbm, hbm, vmem, vmem, vmem, vmem],
        out_specs=(hbm, vmem, vmem, pl.BlockSpec(memory_space=pltpu.SMEM)),
        scratch_shapes=[
            pltpu.VMEM((width, cols), F32),
            pltpu.VMEM((4, size, cols), F32),
            pltpu.VMEM((4, size, cols), F32),
            pltpu.VMEM((2, size, cols), F32),
            pltpu.VMEM((4, size, cols), F32),
            pltpu.VMEM((size, cols), F32),
            pltpu.VMEM((2, 4, size, cols), BF16),
            pltpu.VMEM((2, size, cols), BF16),
            pltpu.VMEM((4, size, cols), F32),
            pltpu.VMEM((cols, cols), F32),
            pltpu.VMEM((cols // 2, cols), F32),
            pltpu.VMEM((5, 16, cols), F32),
            pltpu.VMEM((5, 16, cols), F32),
            dma((4 * H,)), dma((4 * H,)), dma((4 * H,)), dma((4 * H,)), dma((2 * H,)), dma((2 * H,)),
            dma((H,)), dma((H,)), dma((4 * H,)), dma((2 * H,)), dma((4 * H,)),
            dma((8 * count,)), dma((8 * count,)), dma((2 * count,)), dma((2 * count,)),
            dma((count,)), dma((count,)),
            dma((4 * H,)), dma((4 * H,)), dma((4 * H,)), one, one,
            dma((5,)), dma((5,)),
            pltpu.VMEM((rows, width), BF16),
            pltpu.VMEM((width, cols), BF16),
            pltpu.VMEM((rows, cols), BF16),
            dma((8,)), one, one,
            *[pltpu.VMEM((2, 4, *shape), F32) for shape in shapes],
            *[pltpu.VMEM((2, 4, *shape), F32) for shape in shapes],
            *[pltpu.VMEM((2, *shape), F32) for shape in shapes],
        ],
        compiler_params=pltpu.CompilerParams(
            collective_id=0, has_side_effects=True, vmem_limit_bytes=61 * 1024 * 1024
        ),
    )(
        patches, weight, conv_bias, cotangent, row_scale.reshape(-1, 128), col_scale
    )
    return deliver(results)


def solution(mesh):
    in_specs = (P("dp", None), P(None, "mp"), P("mp"), P("dp", "mp"), P(), P("mp"))
    out_specs = (P("dp", "mp"), P("dp", "mp"), P("dp", "mp"), P())
    body = fused if (mesh.shape["dp"], mesh.shape["mp"]) == (8, 4) else shards
    return jax.shard_map(body, mesh=mesh, in_specs=in_specs, out_specs=out_specs, check_vma=False)
```

```python
import functools

import jax
import jax.numpy as jnp
from jax import lax
from jax.experimental import pallas as pl
from jax.experimental.pallas import tpu as pltpu
from jax.sharding import PartitionSpec as P

COUT = 1536
K = 3072
F32 = jnp.float32
BF16 = jnp.bfloat16
MESH = pl.DeviceIdType.MESH


def shards(patches, weight, conv_bias, cotangent, row_scale, col_scale):
    output = (jnp.dot(patches, weight, preferred_element_type=jnp.float32) + conv_bias).astype(
        jnp.bfloat16
    )
    inner_width = patches.shape[1]
    strip_rows = inner_width // lax.axis_size("dp")
    local_grad = lax.dot_general(
        patches, cotangent, (((0,), (0,)), ((), ())), preferred_element_type=jnp.float32
    )
    weighted = local_grad * row_scale[:, None] * col_scale[None, :]
    small_sum = jnp.sum(weighted * weighted)
    column = lax.psum(local_grad, "dp")
    rows_here = lax.dynamic_slice_in_dim(column, lax.axis_index("dp") * strip_rows, strip_rows, 0)
    left_part = lax.dot_general(
        rows_here,
        column,
        (((1,), (1,)), ((), ())),
        precision=lax.Precision.HIGHEST,
        preferred_element_type=jnp.float32,
    )
    left_factor = lax.psum_scatter(left_part / COUT, "mp", scatter_dimension=1, tiled=True)
    full_strip = lax.all_gather(rows_here, "mp", axis=1, tiled=True)
    right_factor = lax.psum_scatter(
        lax.dot_general(
            full_strip,
            rows_here,
            (((0,), (0,)), ((), ())),
            precision=lax.Precision.HIGHEST,
            preferred_element_type=jnp.float32,
        )
        / K,
        "dp",
        scatter_dimension=0,
        tiled=True,
    )
    row_part = lax.dynamic_slice_in_dim(row_scale, lax.axis_index("dp") * strip_rows, strip_rows, 0)
    scaled_rows = rows_here * row_part[:, None] * col_scale[None, :]
    large_sum = jnp.sum(scaled_rows * scaled_rows)
    small_total, large_total = lax.psum((small_sum, large_sum), ("dp", "mp"))
    norm_pair = jnp.stack([small_total, large_total]) / (K * COUT)
    return (output, left_factor, right_factor, norm_pair)


def flip(bit, by):
    return 1 - bit if by else bit


def halves(value):
    high = value.astype(BF16)
    return high, (value - high.astype(F32)).astype(BF16)


def dot3(a, b, dims):
    a_high, a_low = a
    b_high, b_low = b
    dot = functools.partial(
        lax.dot_general, dimension_numbers=(dims, ((), ())), preferred_element_type=F32
    )
    return dot(a_high, b_high) + (dot(a_high, b_low) + dot(a_low, b_high))


GROUPS = (128, 128, 128)
LEVELS = (2, 3)
OUTER = (
    (1, 0, 3), (0, 1, 3), (0, 1, 2), (0, 1, 0), (0, 1, 1), (12, 0), (12, 1), (0, 2, 2), (0, 2, 3), (0, 2, 0),
    (12, 2), (12, 3), (0, 2, 1), (1, 0, 2), (13, 0), (1, 0, 1), (13, 1), (1, 0, 0), (1, 1, 3), (14, 0),
    (1, 1, 2), (1, 1, 0), (4, 0, 0), (4, 0, 1), (1, 1, 1), (4, 0, 2), (6, 0, 1), (1, 2, 2), (4, 0, 3),
    (6, 0, 0), (1, 2, 3), (14, 1), (4, 1, 0), (3, 1), (6, 1, 0), (7, 0, 0), (9, 0, 0, 0), (6, 0, 2),
    (1, 2, 0), (6, 0, 3), (4, 1, 1), (9, 0, 0, 1), (10, 0, 0, 0), (6, 1, 1), (1, 2, 1), (4, 1, 3), (6, 1, 3),
    (7, 0, 3), (3, 0), (9, 0, 0, 3), (10, 0, 0, 3), (7, 0, 1), (4, 1, 2), (6, 1, 2), (9, 0, 0, 2),
    (10, 0, 0, 1), (5, 1), (5, 0), (9, 1, 0, 0), (9, 1, 0, 2), (9, 1, 0, 3), (7, 0, 2), (4, 2, 0), (3, 2),
    (6, 2, 0), (10, 1, 0, 0), (9, 0, 1, 0), (9, 1, 0, 1), (7, 1, 0), (10, 1, 0, 1), (4, 2, 1), (6, 2, 1),
    (9, 0, 1, 1), (10, 1, 0, 3), (10, 1, 0, 2), (5, 2), (9, 1, 1, 1), (7, 1, 1), (9, 1, 1, 0), (14, 2),
    (10, 1, 1, 1), (4, 2, 3), (9, 1, 1, 3), (11, 1, 0), (10, 1, 1, 0), (6, 2, 3), (7, 1, 3), (4, 2, 2),
    (6, 2, 2), (7, 1, 2), (8,), (10, 1, 1, 3), (9, 1, 1, 2), (10, 0, 0, 2), (10, 0, 1, 1), (10, 1, 1, 2),
    (9, 0, 1, 2), (14, 3), (10, 0, 1, 0), (10, 0, 1, 2), (9, 0, 1, 3), (11, 1, 1), (10, 0, 1, 3), (11, 0, 0),
    (14, 4), (13, 2), (11, 0, 1), (15,),
)
INNER = (
    (0, 2, 3), (0, 1, 3), (12, 0), (12, 1), (13, 0), (0, 1, 2), (1, 0, 3), (12, 2), (0, 1, 1), (13, 1),
    (1, 0, 2), (13, 2), (2, 0, 0), (0, 1, 0), (0, 2, 2), (2, 0, 1), (1, 1, 3), (4, 0, 2), (6, 0, 2),
    (1, 1, 2), (4, 0, 3), (6, 0, 3), (2, 1, 1), (6, 1, 1), (2, 1, 0), (3, 1), (3, 0), (9, 0, 0, 1),
    (9, 0, 0, 0), (4, 1, 3), (9, 0, 0, 3), (10, 0, 0, 3), (1, 2, 2), (0, 2, 1), (12, 3), (10, 0, 0, 1),
    (4, 1, 2), (1, 2, 3), (5, 1), (9, 0, 0, 2), (10, 0, 0, 2), (6, 1, 3), (10, 0, 0, 0), (5, 0), (9, 1, 0, 0),
    (9, 1, 0, 2), (0, 2, 0), (10, 1, 0, 2), (9, 1, 0, 1), (2, 2, 1), (9, 1, 0, 3), (7, 0, 3), (10, 1, 0, 0),
    (6, 0, 1), (10, 1, 0, 1), (2, 2, 0), (3, 2), (6, 2, 0), (14, 0), (7, 1, 0), (9, 0, 1, 1), (6, 1, 2),
    (14, 1), (14, 2), (11, 0, 0), (4, 2, 3), (10, 0, 1, 1), (6, 2, 1), (10, 1, 0, 3), (5, 2), (9, 1, 1, 3),
    (9, 1, 1, 1), (9, 1, 1, 0), (7, 1, 1), (4, 2, 2), (6, 2, 3), (7, 1, 3), (10, 1, 1, 1), (11, 1, 0),
    (6, 0, 0), (7, 0, 1), (7, 0, 2), (9, 0, 1, 2), (6, 2, 2), (7, 1, 2), (6, 1, 0), (7, 0, 0), (8,),
    (9, 1, 1, 2), (10, 1, 1, 3), (10, 1, 1, 0), (9, 0, 1, 0), (10, 1, 1, 2), (14, 3), (10, 0, 1, 2),
    (9, 0, 1, 3), (10, 0, 1, 3), (11, 1, 1), (14, 4), (10, 0, 1, 0), (11, 0, 1), (15,),
)

def bounds():
    at = [0]
    for rows in GROUPS:
        at.append(at[-1] + rows)
    return at


def spans_of():
    at = bounds()
    edges = [0] + [at[n] for n in LEVELS]
    spans, levels = [], []
    for low, high in zip(edges[:-1], edges[1:]):
        level = [len(spans)]
        spans.append(((low, high - low), (0, high)))
        if low:
            level.append(len(spans))
            spans.append(((0, low), (low, high - low)))
        levels.append(level)
    return spans, levels


def kernel(
    patches_in, weight_in, bias_in, cot, row_scale, col_scale, output_out, left, right, norms, *scratch
):
    (
        grad, got_x, got_p, got_i, column, other, csplit, osplit, bcol, racc, rgot, nown, ngot,
        s_x, r_x, s_p, r_p, s_i, r_i, s_o, r_o, s_gp, s_gi, r_g,
        s_lc, r_lc, s_ly, r_ly, s_v, r_v, s_b1, s_b2, r_b, s_r, r_r, s_n, r_n,
        patches, weight, output, load, w_load, o_store, s_u,
    ) = scratch[:44]
    spans, levels = spans_of()
    edges = [0] + [bounds()[n] for n in LEVELS]
    count = len(spans)
    parts, cores, over_y = (scratch[44 + i * count:44 + (i + 1) * count] for i in range(3))
    d, m = lax.axis_index("dp"), lax.axis_index("mp")
    x, z = d % 2, d // 2
    z0, z1 = z % 2, z // 2
    c, y = m % 2, m // 2
    zs = (z, z + 1 - 2 * z0, 2 - z1, 3 - 3 * z1)
    px = (d + 1 - 2 * x, m)
    pz = (zs[1] * 2 + x, m)
    pi = ((3 - z) * 2 + x, m)
    pc = (d, m + 1 - 2 * c)
    py = (d, m + 2 - 4 * y)
    inner = (z0 + z1) % 2 == 1
    outer = (z0 + z1) % 2 == 0
    source = m == z
    relay = py[1] == z
    size = rgot.shape[1]
    half = rgot.shape[0]
    at = bounds()
    H = len(GROUPS)
    groups = [pl.ds(at[h], GROUPS[h]) for h in range(H)]

    def strip_at(k, opposite):
        return zs[k] * 2 + (1 - x if opposite else x)

    def strip(k, opposite):
        return pl.ds(pl.multiple_of(strip_at(k, opposite) * size, size), size)

    def strip_group(k, opposite, h):
        first = pl.multiple_of(strip_at(k, opposite) * size + at[h], 32)
        return pl.ds(first, GROUPS[h])

    def copy(src, dst, send, recv, to):
        return pltpu.make_async_remote_copy(
            src_ref=src, dst_ref=dst, send_sem=send, recv_sem=recv, device_id=to, device_id_type=MESH
        )

    barrier = pltpu.get_barrier_semaphore()
    for to in (px, pz, pi, pc, py):
        pl.semaphore_signal(barrier, inc=1, device_id=to, device_id_type=MESH)
    FAR = (3, 2, 1, 0)
    for o in (1, 0):
        for k in FAR:
            rows = strip(k, o)
            pltpu.make_async_copy(
                patches_in.at[:, rows], patches.at[:, rows], load.at[2 * k + o]
            ).start()
    weight_load = pltpu.make_async_copy(weight_in, weight, w_load)
    weight_load.start()
    out_copy = pltpu.make_async_copy(output, output_out, o_store)
    nown[...] = jnp.zeros_like(nown)
    racc[...] = jnp.zeros_like(racc)
    bias = bias_in[...].reshape(1, size)
    col_row = col_scale[...].reshape(1, size)
    col_square = col_row * col_row

    def folded(value, index):
        square = value * value * col_square
        total = jnp.zeros((1, size), F32)
        for b in range(size // 128):
            scale = row_scale[pl.ds(index * (size // 128) + b, 1), :]
            total += dot3(
                halves(scale * scale), halves(square[b * 128:(b + 1) * 128]), ((1,), (0,))
            )
        return total

    def col(k, h):
        return column.at[zs[k], groups[h]]

    hk = [(h, k) for h in range(H) for k in range(4)]
    xc = {
        (h, k): copy(
            grad.at[strip_group(k, 1, h)], got_x.at[k, groups[h]], s_x.at[4 * h + k], r_x.at[4 * h + k], px
        )
        for h, k in hk
    }
    swap = (1, 0, 2, 3)
    to_p = {
        (h, k): copy(
            got_x.at[k, groups[h]], got_p.at[swap[k], groups[h]],
            s_p.at[4 * h + k], r_p.at[4 * h + swap[k]], pz,
        )
        for h, k in hk
    }
    p_in = {(h, k): to_p[h, swap[k]] for h, k in hk}
    to_i = {
        (h, k): copy(
            got_x.at[k, groups[h]], got_i.at[k - 2, groups[h]],
            s_i.at[2 * h + k - 2], r_i.at[2 * h + k - 2], pi,
        )
        for h, k in hk if k >= 2
    }

    def pass_on(k, h, index, send, to):
        return copy(col(k, h), col(k, h), send, r_g.at[4 * h + index], to)

    gp = {(h, k): pass_on(k, h, swap[k], s_gp.at[4 * h + k], pz) for h, k in hk}
    gi = {
        (h, k): pass_on(k, h, k + 2, s_gi.at[2 * h + k], pi) for h in range(H) for k in range(2)
    }
    g_in = {(h, k): pass_on(k, h, k, s_gp.at[0], pz) for h, k in hk}
    o_copy = [copy(col(0, h), other.at[groups[h]], s_o.at[h], r_o.at[h], px) for h in range(H)]

    def b_copy(src, h, k, send, to):
        return copy(src, bcol.at[k, groups[h]], send.at[4 * h + k], r_b.at[4 * h + k], to)

    b_core = {(h, k): b_copy(col(k, h), h, k, s_b1, pc) for h, k in hk}
    b_y = {(h, k): b_copy(col(k, h), h, k, s_b2, py) for h, k in hk}
    b_on = {(h, k): b_copy(bcol.at[k, groups[h]], h, k, s_b1, pc) for h, k in hk}
    wpk = [(w, p, k) for w in range(2) for p in range(count) for k in range(4)]
    lcc = {
        (w, p, k): copy(
            parts[p].at[w, k], cores[p].at[w, k],
            s_lc.at[(w * count + p) * 4 + k], r_lc.at[(w * count + p) * 4 + k], pc,
        )
        for w, p, k in wpk
    }
    lyc = {
        (w, p, k): copy(
            parts[p].at[w, k], over_y[p].at[w], s_ly.at[w * count + p], r_ly.at[w * count + p], py
        )
        for w, p, k in wpk
    }
    at_k = 0
    for k in range(1, 4):
        at_k = at_k + k * (zs[k] == m).astype(jnp.int32)
    left_at = pl.multiple_of(x * size, size)

    def place(p):
        (row, rows), (first, cols) = spans[p]
        return left.at[pl.ds(row, rows), pl.ds(pl.multiple_of(left_at + first, 128), cols)]

    vc = [copy(over_y[p].at[1], place(p), s_v.at[p], r_v.at[p], px) for p in range(count)]
    uc = [pltpu.make_async_copy(over_y[p].at[0], place(p), s_u.at[p]) for p in range(count)]
    rc = copy(racc.at[pl.ds(pl.multiple_of((1 - x) * half, half), half)], rgot, s_r, r_r, px)
    n_to = (pc, pz, pi, py, px)
    nc = [copy(nown.at[i], ngot.at[i], s_n.at[i], r_n.at[i], n_to[i]) for i in range(5)]

    def split(value, ref, g):
        high, low = halves(value)
        ref[0, g, :] = high
        ref[1, g, :] = low

    def zs_dynamic(k):
        low, high = k % 2, k // 2
        near = z + low - 2 * z0 * low
        beyond = 2 - z1 + low * (1 - 2 * z1)
        return near + high * (beyond - near)

    def make_grad(i, _):
        k, opposite = 3 - i % 4, 1 - i // 4
        index = zs_dynamic(k) * 2 + x + opposite - 2 * x * opposite
        rows = pl.ds(pl.multiple_of(index * size, size), size)
        pltpu.make_async_copy(
            patches_in.at[:, rows], patches.at[:, rows], load.at[2 * k + opposite]
        ).wait()
        grad[rows, :] = lax.dot_general(
            patches[:, rows], cot[...], (((0,), (0,)), ((), ())), preferred_element_type=F32
        )

        @pl.when(i == 0)
        def _():
            pl.semaphore_wait(barrier, 5)

        @pl.when(opposite == 1)
        def _():
            first = pl.ds(pl.multiple_of(index * size, size), GROUPS[0])
            copy(grad.at[first], got_x.at[k, groups[0]], s_x.at[k], r_x.at[k], px).start()

        return 0

    def xs(inside, h, k):
        xc[h, k].start()

    def rs(inside, h, k):
        g = groups[h]
        xc[h, k].wait_recv()
        value = got_x[k, g, :] + grad[strip_group(k, 0, h), :]
        if inside:
            p_in[h, k].wait_recv()
            value += got_p[k, g, :]
        got_x[k, g, :] = value
        (to_i if inside else to_p)[h, k].start()

    def fn(inside, h, k):
        g = groups[h]
        xc[h, k].wait_recv()
        p_in[h, k].wait_recv()
        to_i[h, k + 2].wait_recv()
        value = got_x[k, g, :] + grad[strip_group(k, 0, h), :] + got_p[k, g, :] + got_i[k, g, :]
        column[zs[k], g, :] = value
        gp[h, k].start()
        gi[h, k].start()
        split(value, csplit.at[:, k], g)

    def os(inside, h):
        o_copy[h].start()

    def ar(inside, h, k):
        g_in[h, k].wait_recv()
        if inside:
            gp[h, k].start()
        split(column[zs[k], groups[h], :], csplit.at[:, k], groups[h])

    def oth(inside, h):
        o_copy[h].wait_recv()
        split(other[groups[h], :], osplit, groups[h])

    def bs(inside, h, k):
        @pl.when(source)
        def _():
            b_y[h, k].start()
            b_core[h, k].start()
            bcol[k, groups[h], :] = column[zs[k], groups[h], :]

        @pl.when(jnp.logical_not(source))
        def _():
            b_core[h, k].wait_recv()

        @pl.when(relay)
        def _():
            b_on[h, k].start()

    def rt(inside, level, k):
        g = pl.ds(edges[level], edges[level + 1] - edges[level])
        racc[...] += dot3(
            halves(bcol[k, g, :]), (csplit[0, k, g, :], csplit[1, k, g, :]), ((0,), (0,))
        )

    def start_rc(inside):
        rc.start()

    def lu(inside, w, level, k):
        mine = osplit if w else csplit.at[:, 0]
        for p in levels[level]:
            (row, rows), (first, cols) = spans[p]
            g, f = pl.ds(row, rows), pl.ds(first, cols)
            parts[p][w, k] = dot3(
                (mine[0, g, :], mine[1, g, :]), (csplit[0, k, f, :], csplit[1, k, f, :]), ((1,), (1,))
            )

            @pl.when(zs[k] % 2 != c)
            def _():
                lcc[w, p, k].start()

    def rd(inside, w, level, k):
        @pl.when(zs[k] % 2 == c)
        def _():
            for p in levels[level]:
                lcc[w, p, k].wait_recv()
                parts[p][w, k] += cores[p][w, k]

                @pl.when(zs[k] // 2 != y)
                def _():
                    lyc[w, p, k].start()

    def fi(inside, w, level):
        for p in levels[level]:
            lyc[w, p, 0].wait_recv()
            total = (parts[p][w, at_k] + over_y[p][w]) * (1.0 / COUT)
            over_y[p][w] = total
            (vc if w else uc)[p].start()

    def small_step(s, _):
        rows = pl.ds(pl.multiple_of(s * size, size), size)
        nown[0, 0:1, :] += folded(grad[rows, :], s)
        return 0

    def small(inside, i):
        lax.fori_loop(2 * i, 2 * i + 2, small_step, 0)

    def out_step(i, _):
        rows = pl.ds(pl.multiple_of(i * 128, 128), 128)
        value = jnp.dot(patches[rows, :], weight[...], preferred_element_type=F32) + bias
        output[rows, :] = value.astype(BF16)
        return 0

    tiles = patches.shape[0] // 128
    cuts = (0, tiles // 3, 2 * (tiles // 3), tiles)

    def out(inside, i):
        if i == 0:
            weight_load.wait()
        lax.fori_loop(cuts[i], cuts[i + 1], out_step, 0)
        if i == 2:
            out_copy.start()

    def nm(inside, i):
        if i == 0:
            if inside:
                nown[0, 8:9, :] = folded(column[z], strip_at(0, 0)) + folded(
                    column[zs[1]], strip_at(1, 0)
                )
        else:
            nc[i - 1].wait_recv()
            nown[i] = nown[i - 1] + ngot[i - 1]
        nc[i].start()

    def finish(inside):
        nc[4].wait_recv()
        both = nown[4] + ngot[4]
        norms[0] = jnp.sum(both[0:8]) / (K * COUT)
        norms[1] = jnp.sum(both[8:16]) / (K * COUT)
        rc.wait_recv()
        right[...] = (racc[pl.ds(pl.multiple_of(x * half, half), half), :] + rgot[...]) * (1.0 / K)
        for one in vc:
            one.wait_recv()
        for one in uc:
            one.wait()
        out_copy.wait()

    lax.fori_loop(0, 8, make_grad, 0)
    steps = (xs, rs, fn, os, ar, oth, bs, rt, start_rc, lu, rd, fi, small, out, nm, finish)

    @pl.when(outer)
    def _():
        for code, *where in OUTER:
            steps[code](False, *where)

    @pl.when(inner)
    def _():
        for code, *where in INNER:
            steps[code](True, *where)

    sent = [*xc.values(), *o_copy, *vc, rc, *nc]
    for w in range(2):
        for p in range(count):
            sent.append(lyc[w, p, 0])
    for one in sent:
        one.wait_send()

    @pl.when(outer)
    def _():
        for key in hk:
            to_p[key].wait_send()

    @pl.when(inner)
    def _():
        for one in (*to_i.values(), *gp.values(), *gi.values()):
            one.wait_send()

    @pl.when(source)
    def _():
        for key in hk:
            b_y[key].wait_send()
            b_core[key].wait_send()

    @pl.when(relay)
    def _():
        for key in hk:
            b_on[key].wait_send()

    for k in range(4):

        @pl.when(zs[k] % 2 != c)
        def _():
            for w in range(2):
                for p in range(count):
                    lcc[w, p, k].wait_send()


def deliver_kernel(output_in, left_in, right_in, norms_in, output, left, right, norms, sems):
    norms[0] = norms_in[0]
    norms[1] = norms_in[1]
    pairs = ((output_in, output), (left_in, left), (right_in, right))
    copies = [pltpu.make_async_copy(a, b, sems.at[i]) for i, (a, b) in enumerate(pairs)]
    for one in copies:
        one.start()
    for one in copies:
        one.wait()


def deliver(results):
    vmem = pl.BlockSpec(memory_space=pltpu.VMEM)
    hbm = pl.BlockSpec(memory_space=pl.ANY)
    smem = pl.BlockSpec(memory_space=pltpu.SMEM)
    return pl.pallas_call(
        deliver_kernel,
        out_shape=tuple(jax.ShapeDtypeStruct(r.shape, r.dtype) for r in results),
        in_specs=[vmem, vmem, vmem, smem],
        out_specs=(hbm, hbm, hbm, smem),
        scratch_shapes=[pltpu.SemaphoreType.DMA((3,))],
    )(*results)


def fused(patches, weight, conv_bias, cotangent, row_scale, col_scale):
    rows, width = patches.shape
    cols = cotangent.shape[1]
    size = width // 8
    H = len(GROUPS)
    vmem = pl.BlockSpec(memory_space=pltpu.VMEM)
    hbm = pl.BlockSpec(memory_space=pl.ANY)
    dma = pltpu.SemaphoreType.DMA
    one = dma
    spans, _ = spans_of()
    count = len(spans)
    shapes = [(a[1], b[1]) for a, b in spans]
    results = pl.pallas_call(
        kernel,
        out_shape=(
            jax.ShapeDtypeStruct((rows, cols), BF16),
            jax.ShapeDtypeStruct((size, width // 4), F32),
            jax.ShapeDtypeStruct((cols // 2, cols), F32),
            jax.ShapeDtypeStruct((2,), F32),
        ),
        in_specs=[hbm, hbm, vmem, vmem, vmem, vmem],
        out_specs=(hbm, hbm, vmem, pl.BlockSpec(memory_space=pltpu.SMEM)),
        scratch_shapes=[
            pltpu.VMEM((width, cols), F32),
            pltpu.VMEM((4, size, cols), F32),
            pltpu.VMEM((4, size, cols), F32),
            pltpu.VMEM((2, size, cols), F32),
            pltpu.VMEM((4, size, cols), F32),
            pltpu.VMEM((size, cols), F32),
            pltpu.VMEM((2, 4, size, cols), BF16),
            pltpu.VMEM((2, size, cols), BF16),
            pltpu.VMEM((4, size, cols), F32),
            pltpu.VMEM((cols, cols), F32),
            pltpu.VMEM((cols // 2, cols), F32),
            pltpu.VMEM((5, 16, cols), F32),
            pltpu.VMEM((5, 16, cols), F32),
            dma((4 * H,)), dma((4 * H,)), dma((4 * H,)), dma((4 * H,)), dma((2 * H,)), dma((2 * H,)),
            dma((H,)), dma((H,)), dma((4 * H,)), dma((2 * H,)), dma((4 * H,)),
            dma((8 * count,)), dma((8 * count,)), dma((2 * count,)), dma((2 * count,)),
            dma((count,)), dma((count,)),
            dma((4 * H,)), dma((4 * H,)), dma((4 * H,)), one, one,
            dma((5,)), dma((5,)),
            pltpu.VMEM((rows, width), BF16),
            pltpu.VMEM((width, cols), BF16),
            pltpu.VMEM((rows, cols), BF16),
            dma((8,)), one, one, dma((count,)),
            *[pltpu.VMEM((2, 4, *shape), F32) for shape in shapes],
            *[pltpu.VMEM((2, 4, *shape), F32) for shape in shapes],
            *[pltpu.VMEM((2, *shape), F32) for shape in shapes],
        ],
        compiler_params=pltpu.CompilerParams(
            collective_id=0, has_side_effects=True, vmem_limit_bytes=61 * 1024 * 1024
        ),
    )(
        patches, weight, conv_bias, cotangent, row_scale.reshape(-1, 128), col_scale
    )
    return deliver(results)


def solution(mesh):
    in_specs = (P("dp", None), P(None, "mp"), P("mp"), P("dp", "mp"), P(), P("mp"))
    out_specs = (P("dp", "mp"), P("dp", "mp"), P("dp", "mp"), P())
    body = fused if (mesh.shape["dp"], mesh.shape["mp"]) == (8, 4) else shards
    return jax.shard_map(body, mesh=mesh, in_specs=in_specs, out_specs=out_specs, check_vma=False)
```
